32 devices in a mesh: replica: 4 (over x, core), fsdp: 8 (over z, y).
Axes of the slice: x: 2, y: 2, z: 4, core: 2. Of those that a mesh axis runs over, the one named last changes fastest.
Arguments:
- tokens: bfloat16 [4096, 2048], P(('replica', 'fsdp')), may hold values from -6 to 6
- segments: int32 [4096], P(('replica', 'fsdp')), may hold values from 0 to 7, as said below
- cotangent: float32 [4096, 2048], P(('replica', 'fsdp')), may hold values from -6 to 6
- qkv_weight: bfloat16 [2048, 6144], P('fsdp'), may hold values from -1 to 1
- out_weight: bfloat16 [2048, 2048], P('fsdp'), may hold values from -0.125 to 0.125
- gate_up_weight: bfloat16 [2048, 16384], P('fsdp'), may hold values from -0.125 to 0.125
- down_weight: bfloat16 [8192, 2048], P('fsdp'), may hold values from -0.0625 to 0.0625
- q_gain: float32 [2048], replicated, may hold values from 0.5 to 5.5
- k_gain: float32 [2048], replicated, may hold values from 0.5 to 5.5
- attn_gain: float32 [2048], replicated, may hold values from 0.25 to 1.75
- mlp_gain: float32 [2048], replicated, may hold values from 0.25 to 1.75
Outputs:
- result: bfloat16 [4096, 2048], P(('replica', 'fsdp'))
- input_grad: float32 [4096, 2048], P(('replica', 'fsdp'))
- qkv_grad: float32 [2048, 6144], P('fsdp')
- out_grad: float32 [2048, 2048], P('fsdp')
- gate_up_grad: float32 [2048, 16384], P('fsdp')
- down_grad: float32 [8192, 2048], P('fsdp')
- q_gain_grad: float32 [2048], replicated
- k_gain_grad: float32 [2048], replicated
- attn_gain_grad: float32 [2048], replicated
- mlp_gain_grad: float32 [2048], replicated
The draws below stay inside these ranges and needn't reach their ends.
Inputs may be any that keep to these rules, and one draw needn't show every extreme that they name: `segments`: within each sequence of 128 tokens, segment numbers start at 0 and rise by one at each cut; cuts fall only at multiples of 16 tokens, so each piece holds 16 to 128 tokens.
All inputs are finite; a program needn't handle non-finite values.
Results may differ from the reference program's by a relative error of at most 0.02.
The reference program's roundings to bfloat16 on the way count: a program that leaves them out, or rounds other values in their place, can miss the bound.
Values may be sent and summed in bfloat16 or wider, within the bound.
No kernel may reach another device: no remote copies, remote signals or barrier semaphores. Data moves between devices by JAX's collectives and lax.ppermute only.
A program may use at most 576 MiB of HBM per device.

```python
import math
import jax
import jax.numpy as jnp
from jax import lax

D = 2048
HEADS = 16
HEAD_DIM = 128
FF = 8192
SEQ = 128
PIECE = 16
TOKENS = 4096


def draw_tokens(key, part):
    seeded = jax.random.fold_in(key, 11)
    values = jnp.clip(jax.random.normal(seeded, (TOKENS, D), jnp.float32), -6.0, 6.0)
    return values.astype(jnp.bfloat16)


def draw_qkv_weight(key, part):
    seeded = jax.random.fold_in(key, 23)
    fan_scale = D ** (-0.5)
    values = jnp.clip(jax.random.normal(seeded, (D, 3 * D), jnp.float32), -6.0, 6.0) * fan_scale
    return values.astype(jnp.bfloat16)


def draw_q_gain(key, part):
    first = jax.random.fold_in(jax.random.fold_in(key, 31), 0)
    return jnp.exp(jax.random.uniform(first, (D,), jnp.float32, jnp.log(0.5), jnp.log(2.0)))


def draw_k_gain(key, part):
    first = jax.random.fold_in(jax.random.fold_in(key, 37), 0)
    return jnp.exp(jax.random.uniform(first, (D,), jnp.float32, jnp.log(0.5), jnp.log(2.0)))


def draw_segments(key, part):
    seeded = jax.random.fold_in(key, 41)
    seq_count = TOKENS // SEQ
    cut_count = SEQ // PIECE - 1
    cut_flags = jax.random.randint(seeded, (seq_count, cut_count), 0, 2).astype(jnp.int32)
    row_index = lax.broadcasted_iota(jnp.int32, (seq_count, cut_count), 0)
    cut_flags = jnp.where(row_index == 0, 1, cut_flags).astype(jnp.int32)
    piece_ids = jnp.concatenate([jnp.zeros((seq_count, 1), jnp.int32), jnp.cumsum(cut_flags, axis=1).astype(jnp.int32)], axis=1)
    return jnp.repeat(piece_ids, PIECE, axis=1).reshape(TOKENS).astype(jnp.int32)


def block_scale(own_key, shape, shards, least, top_value):
    level = 1.0
    for axis_at, parts in shards:
        draws = jax.random.uniform(jax.random.fold_in(jax.random.fold_in(own_key, 6), axis_at), (parts,), jnp.float32, least / len(shards), top_value / len(shards))
        level = level * jnp.repeat(jnp.exp(draws), shape[axis_at] // parts).reshape((-1,) + (1,) * (len(shape) - 1 - axis_at))
    return level


def bell_draw(rng, dims, scale, reach, cuts=(), kind=jnp.bfloat16):
    values = jax.random.normal(rng, dims, jnp.float32) * scale
    if len(cuts) > 0:
        values = block_scale(rng, dims, cuts, -0.22, 0.18) * values
    return jnp.clip(values, min=-reach, max=reach).astype(kind)


def setup_inputs(seed: int = 0) -> dict:
    key_of = jax.random.split(jax.random.key(seed), 12)
    tokens = draw_tokens(jax.random.fold_in(key_of[11], 71), 0)
    segments = draw_segments(jax.random.fold_in(key_of[11], 71), 0)
    cotangent = bell_draw(key_of[2], (TOKENS, D), 1.0, 6.0, ((0, 32),), jnp.float32)
    qkv_weight = draw_qkv_weight(jax.random.fold_in(key_of[11], 71), 0)
    out_weight = bell_draw(key_of[4], (D, D), D ** -0.5, 0.125, ((0, 8),))
    gate_up_weight = bell_draw(key_of[5], (D, 2 * FF), D ** -0.5, 0.125, ((0, 8),))
    down_weight = bell_draw(key_of[6], (FF, D), FF ** -0.5, 0.0625, ((0, 8),))
    q_gain = draw_q_gain(jax.random.fold_in(key_of[11], 71), 0)
    k_gain = draw_k_gain(jax.random.fold_in(key_of[11], 71), 0)
    attn_gain = jnp.clip(1.0 + 0.15 * jax.random.normal(key_of[9], (D,), jnp.float32), 0.25, 1.75)
    mlp_gain = jnp.clip(1.0 + 0.15 * jax.random.normal(key_of[10], (D,), jnp.float32), 0.25, 1.75)
    return {"tokens": tokens, "segments": segments, "cotangent": cotangent, "qkv_weight": qkv_weight, "out_weight": out_weight, "gate_up_weight": gate_up_weight, "down_weight": down_weight, "q_gain": q_gain, "k_gain": k_gain, "attn_gain": attn_gain, "mlp_gain": mlp_gain}


EPS = 1e-06
THETA = 500000.0
ROWS_DIMS = (((0,), (0,)), ((), ()))
COLS_DIMS = (((1,), (1,)), ((), ()))

def rms_scale(values):
    return lax.rsqrt(lax.optimization_barrier(jnp.mean(values * values, axis=-1, keepdims=True)) + EPS)

def rms_back(values, gain, upstream):
    factor = rms_scale(values)
    normed = values * factor
    d_normed = upstream * gain
    inner = lax.optimization_barrier(jnp.mean(d_normed * normed, axis=-1, keepdims=True))
    return (factor * (d_normed - normed * inner), lax.optimization_barrier(jnp.sum(upstream * normed, axis=0)))

def rope_tables(count):
    half_dim = HEAD_DIM // 2
    freqs = THETA ** (-(2.0 * jnp.arange(half_dim).astype(jnp.float32)) / HEAD_DIM)
    places = (jnp.arange(count, dtype=jnp.int32) % SEQ).astype(jnp.float32)
    angles = places[:, None] * freqs[None, :]
    cosine = jnp.concatenate([jnp.cos(angles), jnp.cos(angles)], axis=1)[:, None, :]
    sine = jnp.concatenate([jnp.sin(angles), jnp.sin(angles)], axis=1)[:, None, :]
    return (cosine, sine)

def rotate(values, cosine, sine):
    half_dim = HEAD_DIM // 2
    turned = jnp.concatenate([-values[..., half_dim:], values[..., :half_dim]], axis=-1)
    return values * cosine + turned * sine

def rotate_back(upstream, cosine, sine):
    half_dim = HEAD_DIM // 2
    scaled = upstream * sine
    turned = jnp.concatenate([scaled[..., half_dim:], -scaled[..., :half_dim]], axis=-1)
    return upstream * cosine + turned

def masked_scores(queries, keys_b, seg_groups):
    scores = jnp.einsum('sqhd,skhd->shqk', queries.astype(jnp.float32), keys_b.astype(jnp.float32))
    scores = scores * HEAD_DIM ** (-0.5)
    index = jnp.arange(SEQ, dtype=jnp.int32)
    causal = index[None, :] <= index[:, None]
    same = seg_groups[:, :, None] == seg_groups[:, None, :]
    allowed = (same & causal[None])[:, None]
    return jnp.where(allowed, scores, -1e+30)

def layer_block(tokens, segments, cotangent, qkv_weight, out_weight, gate_up_weight, down_weight, q_gain, k_gain, attn_gain, mlp_gain):
    count = tokens.shape[0]
    groups = count // SEQ
    qkv = jnp.dot(tokens, qkv_weight, preferred_element_type=jnp.float32)
    q_pre, k_pre, v_pre = (qkv[:, :D], qkv[:, D:2 * D], qkv[:, 2 * D:])
    q_norm = q_pre * rms_scale(q_pre) * q_gain
    k_norm = k_pre * rms_scale(k_pre) * k_gain
    cosine, sine = rope_tables(count)
    q_rot = rotate(q_norm.reshape(count, HEADS, HEAD_DIM), cosine, sine).astype(jnp.bfloat16)
    k_rot = rotate(k_norm.reshape(count, HEADS, HEAD_DIM), cosine, sine).astype(jnp.bfloat16)
    v_b = v_pre.astype(jnp.bfloat16)
    q_grp = q_rot.reshape(groups, SEQ, HEADS, HEAD_DIM)
    k_grp = k_rot.reshape(groups, SEQ, HEADS, HEAD_DIM)
    v_grp = v_b.reshape(groups, SEQ, HEADS, HEAD_DIM)
    seg_groups = segments.reshape(groups, SEQ)
    scores = masked_scores(q_grp, k_grp, seg_groups)
    top = lax.optimization_barrier(jnp.max(scores, axis=-1, keepdims=True))
    lse = top + jnp.log(lax.optimization_barrier(jnp.sum(jnp.exp(scores - top), axis=-1, keepdims=True)))
    prob_b = jnp.exp(scores - lse).astype(jnp.bfloat16)
    attn = jnp.einsum('shqk,skhd->sqhd', prob_b.astype(jnp.float32), v_grp.astype(jnp.float32))
    attn_b = attn.reshape(count, D).astype(jnp.bfloat16)
    pre_attn = jnp.dot(attn_b, out_weight, preferred_element_type=jnp.float32)
    mid = tokens.astype(jnp.float32) + pre_attn * rms_scale(pre_attn) * attn_gain
    mid_b = mid.astype(jnp.bfloat16)
    gate_up = jnp.dot(mid_b, gate_up_weight, preferred_element_type=jnp.float32)
    gate, upper = (gate_up[:, :FF], gate_up[:, FF:])
    sigma = jax.nn.sigmoid(gate)
    hidden_b = (gate * sigma * upper).astype(jnp.bfloat16)
    pre_mlp = jnp.dot(hidden_b, down_weight, preferred_element_type=jnp.float32)
    result = (mid + pre_mlp * rms_scale(pre_mlp) * mlp_gain).astype(jnp.bfloat16)
    d_pre_mlp, mlp_gain_grad = rms_back(pre_mlp, mlp_gain, cotangent)
    dmlp_b = d_pre_mlp.astype(jnp.bfloat16)
    down_grad = lax.dot_general(hidden_b, dmlp_b, ROWS_DIMS, preferred_element_type=jnp.float32)
    d_hidden = lax.dot_general(dmlp_b, down_weight, COLS_DIMS, preferred_element_type=jnp.float32)
    d_gate = d_hidden * upper * sigma * (1.0 + gate * (1.0 - sigma))
    d_upper = d_hidden * gate * sigma
    dgu_b = jnp.concatenate([d_gate, d_upper], axis=1).astype(jnp.bfloat16)
    gate_up_grad = lax.dot_general(mid_b, dgu_b, ROWS_DIMS, preferred_element_type=jnp.float32)
    d_mid = cotangent + lax.dot_general(dgu_b, gate_up_weight, COLS_DIMS, preferred_element_type=jnp.float32)
    d_pre_attn, attn_gain_grad = rms_back(pre_attn, attn_gain, d_mid)
    dattn_in_b = d_pre_attn.astype(jnp.bfloat16)
    out_grad = lax.dot_general(attn_b, dattn_in_b, ROWS_DIMS, preferred_element_type=jnp.float32)
    d_attn_b = lax.dot_general(dattn_in_b, out_weight, COLS_DIMS, preferred_element_type=jnp.float32).astype(jnp.bfloat16)
    d_attn_grp = d_attn_b.reshape(groups, SEQ, HEADS, HEAD_DIM).astype(jnp.float32)
    prob = jnp.exp(masked_scores(q_grp, k_grp, seg_groups) - lse)
    d_value = jnp.einsum('shqk,sqhd->skhd', prob_b.astype(jnp.float32), d_attn_grp)
    d_prob = jnp.einsum('sqhd,skhd->shqk', d_attn_grp, v_grp.astype(jnp.float32))
    delta = lax.optimization_barrier(jnp.sum(prob * d_prob, axis=-1, keepdims=True))
    ds_b = (prob * (d_prob - delta) * HEAD_DIM ** (-0.5)).astype(jnp.bfloat16).astype(jnp.float32)
    dq_rot = jnp.einsum('shqk,skhd->sqhd', ds_b, k_grp.astype(jnp.float32))
    dk_rot = jnp.einsum('shqk,sqhd->skhd', ds_b, q_grp.astype(jnp.float32))
    d_q_norm = rotate_back(dq_rot.reshape(count, HEADS, HEAD_DIM), cosine, sine).reshape(count, D)
    d_k_norm = rotate_back(dk_rot.reshape(count, HEADS, HEAD_DIM), cosine, sine).reshape(count, D)
    d_q_pre, q_gain_grad = rms_back(q_pre, q_gain, d_q_norm)
    d_k_pre, k_gain_grad = rms_back(k_pre, k_gain, d_k_norm)
    dqkv_b = jnp.concatenate([d_q_pre, d_k_pre, d_value.reshape(count, D)], axis=1).astype(jnp.bfloat16)
    qkv_grad = lax.dot_general(tokens, dqkv_b, ROWS_DIMS, preferred_element_type=jnp.float32)
    input_grad = d_mid + lax.dot_general(dqkv_b, qkv_weight, COLS_DIMS, preferred_element_type=jnp.float32)
    grads = (qkv_grad, out_grad, gate_up_grad, down_grad, q_gain_grad, k_gain_grad, attn_gain_grad, mlp_gain_grad)
    return (result, input_grad, grads)

def reference(tokens, segments, cotangent, qkv_weight, out_weight, gate_up_weight, down_weight, q_gain, k_gain, attn_gain, mlp_gain):
    block_rows = math.gcd(TOKENS, 4096)
    blocks = TOKENS // block_rows
    initial = (jnp.zeros((D, 3 * D), jnp.float32), jnp.zeros((D, D), jnp.float32), jnp.zeros((D, 2 * FF), jnp.float32), jnp.zeros((FF, D), jnp.float32), jnp.zeros((D,), jnp.float32), jnp.zeros((D,), jnp.float32), jnp.zeros((D,), jnp.float32), jnp.zeros((D,), jnp.float32))

    def advance(carry, inputs):
        part_tokens, part_segments, part_cot = inputs
        result, input_grad, grads = layer_block(part_tokens, part_segments, part_cot, qkv_weight, out_weight, gate_up_weight, down_weight, q_gain, k_gain, attn_gain, mlp_gain)
        summed = tuple((held + fresh for held, fresh in zip(carry, grads)))
        return (summed, (result, input_grad))
    totals, (results, in_grads) = lax.scan(advance, initial, (tokens.reshape(blocks, block_rows, D), segments.reshape(blocks, block_rows), cotangent.reshape(blocks, block_rows, D)))
    return (results.reshape(TOKENS, D), in_grads.reshape(TOKENS, D), totals[0], totals[1], totals[2], totals[3], totals[4], totals[5], totals[6], totals[7])
```

```python
import jax
import jax.numpy as jnp
from jax import lax
from jax.experimental import pallas as pl
from jax.experimental.pallas import tpu as pltpu
from jax.sharding import PartitionSpec as P

D = 2048
HEADS = 16
HEAD_DIM = 128
FF = 8192
SEQ = 128


EPS = 1e-06
THETA = 500000.0
ROWS_DIMS = (((0,), (0,)), ((), ()))
COLS_DIMS = (((1,), (1,)), ((), ()))


def rms_scale(values):
    return lax.rsqrt(jnp.mean(values * values, axis=-1, keepdims=True) + EPS)


def rms_back(values, gain, upstream):
    factor = rms_scale(values)
    normed = values * factor
    d_normed = upstream * gain
    inner = jnp.mean(d_normed * normed, axis=-1, keepdims=True)
    return (factor * (d_normed - normed * inner), jnp.sum(upstream * normed, axis=0))


def rope_tables(count):
    half_dim = HEAD_DIM // 2
    freqs = THETA ** (-(2.0 * jnp.arange(half_dim).astype(jnp.float32)) / HEAD_DIM)
    places = (jnp.arange(count, dtype=jnp.int32) % SEQ).astype(jnp.float32)
    angles = places[:, None] * freqs[None, :]
    cosine = jnp.concatenate([jnp.cos(angles), jnp.cos(angles)], axis=1)[:, None, :]
    sine = jnp.concatenate([jnp.sin(angles), jnp.sin(angles)], axis=1)[:, None, :]
    return (cosine, sine)


def rotate(values, cosine, sine):
    half_dim = HEAD_DIM // 2
    turned = jnp.concatenate([-values[..., half_dim:], values[..., :half_dim]], axis=-1)
    return values * cosine + turned * sine


def rotate_back(upstream, cosine, sine):
    half_dim = HEAD_DIM // 2
    scaled = upstream * sine
    turned = jnp.concatenate([scaled[..., half_dim:], -scaled[..., :half_dim]], axis=-1)
    return upstream * cosine + turned


def masked_scores(queries, keys_b, seg_groups):
    scores = jnp.einsum("sqhd,skhd->shqk", queries, keys_b, preferred_element_type=jnp.float32)
    scores = scores * HEAD_DIM ** (-0.5)
    index = jnp.arange(SEQ, dtype=jnp.int32)
    causal = index[None, :] <= index[:, None]
    same = seg_groups[:, :, None] == seg_groups[:, None, :]
    allowed = (same & causal[None])[:, None]
    return jnp.where(allowed, scores, -1e30)


def fold_with(activations, incoming):
    return jnp.dot(activations, incoming, preferred_element_type=jnp.float32)


def back_with(upstream, incoming):
    return lax.dot_general(upstream, incoming, COLS_DIMS, preferred_element_type=jnp.float32)


def weight_grad(activations, upstream):
    return lax.psum_scatter(
        lax.dot_general(
            activations, upstream, ROWS_DIMS, preferred_element_type=jnp.float32
        ).astype(jnp.bfloat16),
        "fsdp",
        scatter_dimension=0,
        tiled=True,
    ).astype(jnp.float32)


def gathered(
    tokens,
    segments,
    cotangent,
    qkv_weight,
    out_weight,
    gate_up_weight,
    down_weight,
    q_gain,
    k_gain,
    attn_gain,
    mlp_gain,
):
    count = tokens.shape[0]
    groups = count // SEQ
    qkv = fold_with(tokens, lax.all_gather(qkv_weight, "fsdp", axis=0, tiled=True))
    q_pre, k_pre, v_pre = (qkv[:, :D], qkv[:, D : 2 * D], qkv[:, 2 * D :])
    q_norm = q_pre * rms_scale(q_pre) * q_gain
    k_norm = k_pre * rms_scale(k_pre) * k_gain
    cosine, sine = rope_tables(count)
    q_rot = rotate(q_norm.reshape(count, HEADS, HEAD_DIM), cosine, sine).astype(jnp.bfloat16)
    k_rot = rotate(k_norm.reshape(count, HEADS, HEAD_DIM), cosine, sine).astype(jnp.bfloat16)
    v_b = v_pre.astype(jnp.bfloat16)
    q_grp = q_rot.reshape(groups, SEQ, HEADS, HEAD_DIM)
    k_grp = k_rot.reshape(groups, SEQ, HEADS, HEAD_DIM)
    v_grp = v_b.reshape(groups, SEQ, HEADS, HEAD_DIM)
    seg_groups = segments.reshape(groups, SEQ)
    scores = masked_scores(q_grp, k_grp, seg_groups)
    top = jnp.max(scores, axis=-1, keepdims=True)
    lse = top + jnp.log(jnp.sum(jnp.exp(scores - top), axis=-1, keepdims=True))
    prob_b = jnp.exp(scores - lse).astype(jnp.bfloat16)
    attn = jnp.einsum("shqk,skhd->sqhd", prob_b, v_grp, preferred_element_type=jnp.float32)
    attn_b = attn.reshape(count, D).astype(jnp.bfloat16)
    pre_attn = fold_with(attn_b, lax.all_gather(out_weight, "fsdp", axis=0, tiled=True))
    mid = tokens.astype(jnp.float32) + pre_attn * rms_scale(pre_attn) * attn_gain
    mid_b = mid.astype(jnp.bfloat16)
    gate_up = fold_with(mid_b, lax.all_gather(gate_up_weight, "fsdp", axis=0, tiled=True))
    gate, upper = (gate_up[:, :FF], gate_up[:, FF:])
    sigma = jax.nn.sigmoid(gate)
    hidden_b = (gate * sigma * upper).astype(jnp.bfloat16)
    pre_mlp = fold_with(hidden_b, lax.all_gather(down_weight, "fsdp", axis=0, tiled=True))
    result = (mid + pre_mlp * rms_scale(pre_mlp) * mlp_gain).astype(jnp.bfloat16)
    d_pre_mlp, mlp_gain_part = rms_back(pre_mlp, mlp_gain, cotangent)
    dmlp_b = d_pre_mlp.astype(jnp.bfloat16)
    down_part = weight_grad(hidden_b, dmlp_b)
    d_hidden = back_with(dmlp_b, lax.all_gather(down_weight, "fsdp", axis=0, tiled=True))
    d_gate = d_hidden * upper * sigma * (1.0 + gate * (1.0 - sigma))
    d_upper = d_hidden * gate * sigma
    dgu_b = jnp.concatenate([d_gate, d_upper], axis=1).astype(jnp.bfloat16)
    gate_up_part = weight_grad(mid_b, dgu_b)
    d_mid = cotangent + back_with(dgu_b, lax.all_gather(gate_up_weight, "fsdp", axis=0, tiled=True))
    d_pre_attn, attn_gain_part = rms_back(pre_attn, attn_gain, d_mid)
    dattn_in_b = d_pre_attn.astype(jnp.bfloat16)
    out_part = weight_grad(attn_b, dattn_in_b)
    d_attn_b = back_with(dattn_in_b, lax.all_gather(out_weight, "fsdp", axis=0, tiled=True)).astype(
        jnp.bfloat16
    )
    d_attn_grp = d_attn_b.reshape(groups, SEQ, HEADS, HEAD_DIM)
    prob = jnp.exp(masked_scores(q_grp, k_grp, seg_groups) - lse)
    d_value = jnp.einsum("shqk,sqhd->skhd", prob_b, d_attn_grp, preferred_element_type=jnp.float32)
    d_prob = jnp.einsum("sqhd,skhd->shqk", d_attn_grp, v_grp, preferred_element_type=jnp.float32)
    delta = jnp.sum(prob * d_prob, axis=-1, keepdims=True)
    ds_b = (prob * (d_prob - delta) * HEAD_DIM ** (-0.5)).astype(jnp.bfloat16)
    dq_rot = jnp.einsum("shqk,skhd->sqhd", ds_b, k_grp, preferred_element_type=jnp.float32)
    dk_rot = jnp.einsum("shqk,sqhd->skhd", ds_b, q_grp, preferred_element_type=jnp.float32)
    d_q_norm = rotate_back(dq_rot.reshape(count, HEADS, HEAD_DIM), cosine, sine).reshape(count, D)
    d_k_norm = rotate_back(dk_rot.reshape(count, HEADS, HEAD_DIM), cosine, sine).reshape(count, D)
    d_q_pre, q_gain_part = rms_back(q_pre, q_gain, d_q_norm)
    d_k_pre, k_gain_part = rms_back(k_pre, k_gain, d_k_norm)
    dqkv_b = jnp.concatenate([d_q_pre, d_k_pre, d_value.reshape(count, D)], axis=1).astype(
        jnp.bfloat16
    )
    qkv_part = weight_grad(tokens, dqkv_b)
    input_grad = d_mid + back_with(dqkv_b, lax.all_gather(qkv_weight, "fsdp", axis=0, tiled=True))
    qkv_grad, out_grad, gate_up_grad, down_grad = (
        lax.psum(qkv_part.astype(jnp.bfloat16), "replica").astype(jnp.float32),
        lax.psum(out_part.astype(jnp.bfloat16), "replica").astype(jnp.float32),
        lax.psum(gate_up_part.astype(jnp.bfloat16), "replica").astype(jnp.float32),
        lax.psum(down_part.astype(jnp.bfloat16), "replica").astype(jnp.float32),
    )
    q_gain_grad, k_gain_grad, attn_gain_grad, mlp_gain_grad = lax.psum(
        (q_gain_part, k_gain_part, attn_gain_part, mlp_gain_part), ("replica", "fsdp")
    )
    return (
        result,
        input_grad,
        qkv_grad,
        out_grad,
        gate_up_grad,
        down_grad,
        q_gain_grad,
        k_gain_grad,
        attn_gain_grad,
        mlp_gain_grad,
    )


def swap_pairs(count, bits):
    return [(i, i ^ bits) for i in range(count)]


def lane_pairs(hops):
    return [(2 * a + y, 2 * b + y) for a, b in hops for y in range(2)]


OUTER_IN = ((3, 2), (0, 1))
INNER_OUT = ((2, 3), (1, 0))
MIDDLE = ((1, 2), (2, 1))


def hop(value, bits):
    return lax.ppermute(value, "fsdp", swap_pairs(8, bits))


def lane(value, hops):
    return lax.ppermute(value, "fsdp", lane_pairs(hops))


def spread(own):
    s1 = hop(own, 1)
    s2 = hop(own, 2)
    near = lane(own, MIDDLE)
    s3 = hop(s2, 1)
    far = lane(s2, MIDDLE)
    s4 = far + lane(near, INNER_OUT)
    s5 = hop(s4, 1)
    s6 = near + lane(far, INNER_OUT)
    s7 = hop(s6, 1)
    return [own, s1, s2, s3, s4, s5, s6, s7]


def collect(make):
    held = {}
    for j in (3, 2, 1, 0):
        part = make(j)
        held[j] = part[0] + hop(part[1].astype(jnp.bfloat16), 1).astype(jnp.float32)
    narrow = lambda value: value.astype(jnp.bfloat16)
    wide = lambda value: value.astype(jnp.float32)
    far = held[2] + wide(lane(narrow(held[3]), OUTER_IN))
    near = held[3] + wide(lane(narrow(held[2]), OUTER_IN))
    next_to = held[1] + wide(lane(narrow(far), MIDDLE))
    return held[0] + wide(lane(narrow(near), MIDDLE)) + wide(hop(narrow(next_to), 2))


BF16 = jnp.bfloat16
F32 = jnp.float32


def core_hop(value):
    return lax.ppermute(value, "replica", swap_pairs(4, 1))


def chip_hop(value):
    return lax.ppermute(value, "replica", swap_pairs(4, 2))


def absolute(blocks, index):
    held = jnp.zeros((len(blocks),) + blocks[0].shape, blocks[0].dtype)
    for k, block in enumerate(blocks):
        held = lax.dynamic_update_slice_in_dim(held, block[None], index ^ k, axis=0)
    return held


def swap_blocks(block_for):
    return [block_for(0)] + [hop(block_for(k), k) for k in range(1, 8)]


def replica_gather(block):
    across = chip_hop(block)
    return [block, core_hop(block), across, core_hop(across)]


def call(body, grid, ins, outs, shapes, flops=0, moved=0, scalars=0):
    return pl.pallas_call(
        body,
        grid_spec=pltpu.PrefetchScalarGridSpec(
            num_scalar_prefetch=scalars, grid=grid, in_specs=ins, out_specs=outs
        ),
        out_shape=shapes,
        compiler_params=pltpu.CompilerParams(
            dimension_semantics=("arbitrary",) * len(grid), vmem_limit_bytes=32 * 1024 * 1024
        ),
        cost_estimate=pl.CostEstimate(flops=flops, bytes_accessed=moved, transcendentals=0),
    )


def sum_body(inverse, *refs):
    out = refs[-1]
    for k in range(8):
        total = refs[0][k]
        for bits in range(1, 8):
            total = total + refs[bits][k ^ bits]
        total = total / D
        out[k] = lax.rsqrt(total + EPS) if inverse else total


def slot_mean(values, inverse):
    parts = [values] + [hop(values, bits) for bits in range(1, 8)]
    spec = pl.BlockSpec(values.shape, lambda i: (0, 0, 0))
    return call(
        lambda *refs: sum_body(inverse, *refs),
        (1,),
        [spec] * 8,
        spec,
        jax.ShapeDtypeStruct(values.shape, F32),
    )(*parts)


def diagonal():
    down = lax.broadcasted_iota(jnp.int32, (SEQ, SEQ), 0)
    right = lax.broadcasted_iota(jnp.int32, (SEQ, SEQ), 1)
    return down, right


def upright(row):
    down, right = diagonal()
    return jnp.sum(jnp.where(down == right, row, 0.0), axis=1, keepdims=True)


def flat(column):
    down, right = diagonal()
    return jnp.sum(jnp.where(down == right, column, 0.0), axis=0, keepdims=True)


def nt(a, b):
    return lax.dot_general(a, b, COLS_DIMS, preferred_element_type=F32)


def tn(a, b):
    return lax.dot_general(a, b, ROWS_DIMS, preferred_element_type=F32)


def allowed_pairs(seg_ref):
    down, right = diagonal()
    row = seg_ref[0].astype(F32)
    return (upright(row) == row) & (right <= down)


def softmax(q, k, allowed):
    scores = jnp.where(allowed, nt(q, k) * HEAD_DIM ** (-0.5), -1e30)
    top = jnp.max(scores, axis=1, keepdims=True)
    lse = top + jnp.log(jnp.sum(jnp.exp(scores - top), axis=1, keepdims=True))
    return jnp.exp(scores - lse)


def attend_body(qkv_ref, fac_ref, seg_ref, gain_ref, cos_ref, sin_ref, rot_ref, attn_ref):
    wide = attn_ref.shape[1]
    allowed = allowed_pairs(seg_ref)
    cosine, sine = cos_ref[...], sin_ref[...]
    factor = [upright(fac_ref[0, i : i + 1, :]) for i in range(2)]
    for h in range(wide // HEAD_DIM):
        turned = []
        for i in range(2):
            at = slice(i * wide + h * HEAD_DIM, i * wide + (h + 1) * HEAD_DIM)
            value = qkv_ref[:, at] * factor[i] * gain_ref[i : i + 1, h * HEAD_DIM : (h + 1) * HEAD_DIM]
            value = value * cosine + pltpu.roll(value, HEAD_DIM // 2, 1) * sine
            turned.append(value.astype(BF16))
            rot_ref[:, at] = turned[i]
        at = slice(2 * wide + h * HEAD_DIM, 2 * wide + (h + 1) * HEAD_DIM)
        value_b = qkv_ref[:, at].astype(BF16)
        rot_ref[:, at] = value_b
        prob_b = softmax(turned[0], turned[1], allowed).astype(BF16)
        attn = jnp.dot(prob_b, value_b, preferred_element_type=F32)
        attn_ref[:, h * HEAD_DIM : (h + 1) * HEAD_DIM] = attn.astype(BF16)


def attend_back_body(
    rot_ref, up_ref, qkv_ref, fac_ref, seg_ref, gain_ref, cos_ref, sin_ref, dn_ref, dv_ref, inner_ref, sum_ref
):
    wide = up_ref.shape[1]
    allowed = allowed_pairs(seg_ref)
    cosine, sine = cos_ref[...], sin_ref[...]
    factor = [upright(fac_ref[0, i : i + 1, :]) for i in range(2)]
    inner = [0.0, 0.0]

    @pl.when(pl.program_id(0) == 0)
    def _():
        sum_ref[...] = jnp.zeros_like(sum_ref)

    for h in range(wide // HEAD_DIM):
        own = slice(h * HEAD_DIM, (h + 1) * HEAD_DIM)
        q, k, v = (
            rot_ref[:, i * wide + h * HEAD_DIM : i * wide + (h + 1) * HEAD_DIM] for i in range(3)
        )
        up = up_ref[:, own]
        prob = softmax(q, k, allowed)
        dv_ref[:, own] = tn(prob.astype(BF16), up).astype(BF16)
        d_prob = nt(up, v)
        delta = jnp.sum(prob * d_prob, axis=1, keepdims=True)
        ds_b = (prob * (d_prob - delta) * HEAD_DIM ** (-0.5)).astype(BF16)
        back = (jnp.dot(ds_b, k, preferred_element_type=F32), tn(ds_b, q))
        for i in range(2):
            at = slice(i * wide + h * HEAD_DIM, i * wide + (h + 1) * HEAD_DIM)
            d_norm = back[i] * cosine + pltpu.roll(back[i] * sine, HEAD_DIM // 2, 1)
            dn_ref[:, at] = d_norm
            unit = qkv_ref[:, at] * factor[i]
            inner[i] = inner[i] + jnp.sum(
                d_norm * gain_ref[i : i + 1, own] * unit, axis=1, keepdims=True
            )
            sum_ref[i : i + 1, own] += jnp.sum(d_norm * unit, axis=0, keepdims=True)
    for i in range(2):
        inner_ref[0, i : i + 1, :] = flat(inner[i])


def norm_back_body(dn_ref, dv_ref, qkv_ref, fac_ref, mean_ref, gain_ref, out_ref):
    wide = dv_ref.shape[1]
    for i in range(2):
        at = slice(i * wide, (i + 1) * wide)
        factor = upright(fac_ref[0, i : i + 1, :])
        mean = upright(mean_ref[0, i : i + 1, :])
        unit = qkv_ref[:, at] * factor
        value = factor * (dn_ref[:, at] * gain_ref[i : i + 1, :] - unit * mean)
        out_ref[:, at] = value.astype(BF16)
    out_ref[:, 2 * wide :] = dv_ref[...]


def gate_up_body(copy_ref, *refs):
    out = refs[-1]
    width = refs[0].shape[2]
    for m in range(4):
        start = pl.multiple_of((copy_ref[0] ^ m) * width, width)
        out[:, pl.ds(start, width)] = refs[m][0].astype(F32)


def qkv_body(copy_ref, *refs):
    out = refs[-1]
    members, height, width = refs[0].shape
    for m in range(4):
        start = pl.multiple_of((copy_ref[0] ^ m) * height, height)
        for i in range(members):
            out[pl.ds(start, height), i * width : (i + 1) * width] = refs[m][i].astype(F32)


def halves(left, right, core, height):
    own = lax.dynamic_slice_in_dim(left, core * height, height, axis=1)
    other = lax.dynamic_slice_in_dim(left, (1 - core) * height, height, axis=1)
    return (tn(own, right) + core_hop(tn(other, right).astype(BF16)).astype(F32)).astype(BF16)


def join_halves(pair_b, other, core):
    total = (pair_b.astype(F32) + other.astype(F32)).astype(BF16)
    back = core_hop(total)
    first = jnp.where(core == 0, total, back)
    second = jnp.where(core == 0, back, total)
    return jnp.concatenate([first, second]).astype(F32)


def quarters(part_for):
    third = core_hop(part_for(3).astype(BF16))
    first = core_hop(part_for(1).astype(BF16))
    return part_for(0) + first.astype(F32), (part_for(2) + third.astype(F32)).astype(BF16)


tie = lax.optimization_barrier


def tensor_split(
    tokens,
    segments,
    cotangent,
    qkv_weight,
    out_weight,
    gate_up_weight,
    down_weight,
    q_gain,
    k_gain,
    attn_gain,
    mlp_gain,
):
    members, copies = 8, 4
    rows = tokens.shape[0]
    count = members * rows
    wide = D // members
    units = FF // members
    quarter = units // copies
    place = lax.axis_index("fsdp")
    copy = lax.axis_index("replica")
    core = copy % 2
    owned = qkv_weight.shape[0]
    sub = owned // copies
    copy_at = copy.astype(jnp.int32).reshape(1)

    def qkv_block(k):
        parts = [
            lax.dynamic_slice(qkv_weight, (copy * sub, i * D + (place ^ k) * wide), (sub, wide))
            for i in range(3)
        ]
        return jnp.concatenate(parts, axis=1)

    def gate_up_block(k):
        parts = [
            lax.dynamic_slice_in_dim(
                gate_up_source, i * FF + (place ^ k) * units + copy * quarter, quarter, axis=1
            )
            for i in range(2)
        ]
        return jnp.concatenate(parts, axis=1)

    mine = lambda gain: lax.dynamic_slice_in_dim(gain, place * wide, wide)
    gain_own = jnp.stack([mine(q_gain), mine(k_gain)])

    piece = absolute(swap_blocks(qkv_block), place)
    seg_slots = jnp.concatenate([segments[None]] + [hop(segments[None], k) for k in range(1, members)])
    seg_slots = seg_slots.reshape(members, 1, rows)
    token_slots = spread(tokens)
    pieces = absolute(replica_gather(piece), copy)
    qkv_cols = pieces.transpose(1, 0, 2, 3).reshape(D, 3 * wide)
    cosine, sine = rope_tables(rows)
    sign = jnp.where(jnp.arange(HEAD_DIM) < HEAD_DIM // 2, -1.0, 1.0)
    cosine, sine = cosine[:, 0], sine[:, 0] * sign

    gate_up_source, token_slots[6] = tie((gate_up_weight, token_slots[6]))
    token_all = jnp.concatenate(token_slots)
    qkv = fold_with(token_all, qkv_cols)
    gate_up_piece = absolute(swap_blocks(gate_up_block), place).reshape(D, 2 * quarter)

    q_pre, k_pre = (qkv[:, :wide], qkv[:, wide : 2 * wide])
    squares = [jnp.sum(value * value, axis=1).reshape(members, rows) for value in (q_pre, k_pre)]
    factors = slot_mean(jnp.stack(squares, axis=1), True)
    slab = lambda width: pl.BlockSpec((rows, width), lambda i: (i, 0))
    line = lambda n: pl.BlockSpec((1, n, rows), lambda i: (i, 0, 0))
    whole = lambda shape: pl.BlockSpec(shape, lambda i: (0,) * len(shape))
    tables = [whole((2, wide)), whole((rows, HEAD_DIM)), whole((rows, HEAD_DIM))]
    rot, attn_b = call(
        attend_body,
        (members,),
        [slab(3 * wide), line(2), line(1)] + tables,
        [slab(3 * wide), slab(wide)],
        [jax.ShapeDtypeStruct((count, 3 * wide), BF16), jax.ShapeDtypeStruct((count, wide), BF16)],
        flops=4 * count * rows * wide,
        moved=count * wide * 20,
    )(qkv, factors, seg_slots, gain_own, cosine, sine)

    span = 2 * rows
    rows_of = lambda value, j: value[j * span : (j + 1) * span]
    pre_attn = collect(lambda j: fold_with(rows_of(attn_b, j), out_weight).reshape(2, rows, D))
    gate_up_all = replica_gather(gate_up_piece)
    pre_attn, gate_up_all = tie((pre_attn, gate_up_all))
    gate_up_cols = absolute(gate_up_all, copy)
    mid = tokens.astype(F32) + pre_attn * rms_scale(pre_attn) * attn_gain
    mid_b = mid.astype(BF16)

    mid_all = jnp.concatenate(spread(mid_b))
    gate_up = [fold_with(mid_all, gate_up_cols[c]) for c in range(copies)]
    gate = [value[:, :quarter] for value in gate_up]
    upper = [value[:, quarter:] for value in gate_up]
    sigma = [jax.nn.sigmoid(value) for value in gate]
    hidden_b = jnp.concatenate(
        [(g * s * u).astype(BF16) for g, s, u in zip(gate, sigma, upper)], axis=1
    )
    pre_mlp = collect(lambda j: fold_with(rows_of(hidden_b, j), down_weight).reshape(2, rows, D))
    result = (mid + pre_mlp * rms_scale(pre_mlp) * mlp_gain).astype(BF16)
    d_pre_mlp, mlp_gain_part = rms_back(pre_mlp, mlp_gain, cotangent)
    dmlp_b = d_pre_mlp.astype(BF16)

    dmlp_all = jnp.concatenate(spread(dmlp_b))
    d_hidden = back_with(dmlp_all, down_weight)
    dgu = []
    for c in range(copies):
        d_h = d_hidden[:, c * quarter : (c + 1) * quarter]
        d_gate = d_h * upper[c] * sigma[c] * (1.0 + gate[c] * (1.0 - sigma[c]))
        d_upper = d_h * gate[c] * sigma[c]
        dgu.append(jnp.concatenate([d_gate, d_upper], axis=1).astype(BF16))

    def d_mid_part(j):
        total = back_with(rows_of(dgu[0], j), gate_up_cols[0])
        for c in range(1, copies):
            total = total + back_with(rows_of(dgu[c], j), gate_up_cols[c])
        return total.reshape(2, rows, D)

    d_mid = cotangent + collect(d_mid_part)
    dgu_all = jnp.stack(dgu)
    gate_up_own, gate_up_sent = quarters(
        lambda m: tn(mid_all, lax.dynamic_index_in_dim(dgu_all, copy ^ m, axis=0, keepdims=False))
    )
    d_mid, gate_up_own, gate_up_sent = tie((d_mid, gate_up_own, gate_up_sent))
    gate_up_part = (gate_up_own + chip_hop(gate_up_sent).astype(F32)).astype(BF16)
    down_pair = halves(hidden_b, dmlp_all, core, units // 2)

    d_pre_attn, attn_gain_part = rms_back(pre_attn, attn_gain, d_mid)
    dattn_all = jnp.concatenate(spread(d_pre_attn.astype(BF16)))
    dattn_all, gate_up_part, down_pair = tie((dattn_all, gate_up_part, down_pair))
    gate_up_block_for = lambda k: lax.dynamic_slice_in_dim(
        gate_up_part, (place ^ k) * owned, owned, axis=0
    )
    gate_up_blocks = swap_blocks(gate_up_block_for)
    down_other = chip_hop(down_pair)
    d_attn_b = back_with(dattn_all, out_weight).astype(BF16)
    d_norm, d_value, inner, gain_sums = call(
        attend_back_body,
        (members,),
        [slab(3 * wide), slab(wide), slab(3 * wide), line(2), line(1)] + tables,
        [slab(2 * wide), slab(wide), line(2), whole((2, wide))],
        [
            jax.ShapeDtypeStruct((count, 2 * wide), F32),
            jax.ShapeDtypeStruct((count, wide), BF16),
            jax.ShapeDtypeStruct((members, 2, rows), F32),
            jax.ShapeDtypeStruct((2, wide), F32),
        ],
        flops=10 * count * rows * wide,
        moved=count * wide * 30,
    )(rot, d_attn_b, qkv, factors, seg_slots, gain_own, cosine, sine)
    means = slot_mean(inner, False)
    out_pair = halves(attn_b, dattn_all, core, wide // 2)
    dqkv_b = call(
        norm_back_body,
        (members,),
        [slab(2 * wide), slab(wide), slab(3 * wide), line(2), line(2), whole((2, wide))],
        slab(3 * wide),
        jax.ShapeDtypeStruct((count, 3 * wide), BF16),
        flops=count * wide * 10,
        moved=count * wide * 28,
    )(d_norm, d_value, qkv, factors, means, gain_own)
    dqkv_b, down_other, gate_up_blocks = tie((dqkv_b, down_other, gate_up_blocks))
    out_other = chip_hop(out_pair)
    gate_up_parts = replica_gather(absolute(gate_up_blocks, place))
    down_grad = join_halves(down_pair, down_other, core)

    qkv_full = tn(token_all, dqkv_b).reshape(members, copies, sub, 3 * wide)
    qkv_own, qkv_sent = quarters(
        lambda m: lax.dynamic_index_in_dim(qkv_full, copy ^ m, axis=1, keepdims=False)
    )
    qkv_part = (qkv_own + chip_hop(qkv_sent).astype(F32)).astype(BF16)
    qkv_blocks = swap_blocks(
        lambda k: lax.dynamic_index_in_dim(qkv_part, place ^ k, axis=0, keepdims=False)
    )
    input_grad = d_mid + collect(
        lambda j: back_with(rows_of(dqkv_b, j), qkv_cols).reshape(2, rows, D)
    )
    out_grad = join_halves(out_pair, out_other, core)
    gate_up_grad = call(
        gate_up_body,
        (2, members),
        [pl.BlockSpec((1, owned, quarter), lambda h, i, c: (i, 0, h))] * copies,
        pl.BlockSpec((owned, units), lambda h, i, c: (0, h * members + i)),
        jax.ShapeDtypeStruct((owned, 2 * FF), F32),
        moved=owned * FF * 12,
        scalars=1,
    )(copy_at, *gate_up_parts)
    qkv_grad = call(
        qkv_body,
        (3,),
        [pl.BlockSpec((members, sub, wide), lambda i, c: (0, 0, i))] * copies,
        pl.BlockSpec((owned, D), lambda i, c: (0, i)),
        jax.ShapeDtypeStruct((owned, 3 * D), F32),
        moved=owned * D * 18,
        scalars=1,
    )(copy_at, *replica_gather(absolute(qkv_blocks, place)))

    blank = jnp.zeros((2, D), F32)
    gains = jnp.concatenate(
        [
            lax.dynamic_update_slice_in_dim(blank, gain_sums, place * wide, axis=1),
            attn_gain_part[None],
            mlp_gain_part[None],
        ]
    )
    for bits in (1, 2, 4):
        gains = gains + hop(gains, bits)
    gains = gains + core_hop(gains)
    gains = gains + chip_hop(gains)
    return (
        result,
        input_grad,
        qkv_grad,
        out_grad,
        gate_up_grad,
        down_grad,
        gains[0],
        gains[1],
        gains[2],
        gains[3],
    )


def solution(mesh):
    def per_device(*arrays):
        fits = mesh.shape["fsdp"] == 8 and mesh.shape["replica"] == 4 and arrays[0].shape[0] == SEQ
        return (tensor_split if fits else gathered)(*arrays)


    placed = (
        P(("replica", "fsdp"), None),
        P(("replica", "fsdp")),
        P(("replica", "fsdp"), None),
        P("fsdp", None),
        P("fsdp", None),
        P("fsdp", None),
        P("fsdp", None),
        P(),
        P(),
        P(),
        P(),
    )
    return jax.shard_map(
        per_device,
        mesh=mesh,
        in_specs=placed,
        out_specs=(
            P(("replica", "fsdp"), None),
            P(("replica", "fsdp"), None),
            P("fsdp", None),
            P("fsdp", None),
            P("fsdp", None),
            P("fsdp", None),
            P(),
            P(),
            P(),
            P(),
        ),
        check_vma=False,
    )
```

```python
import jax
import jax.numpy as jnp
from jax import lax
from jax.experimental import pallas as pl
from jax.experimental.pallas import tpu as pltpu
from jax.sharding import PartitionSpec as P


D = 2048
HEADS = 16
HEAD_DIM = 128
FF = 8192
SEQ = 128


EPS = 1e-06
THETA = 500000.0
ROWS_DIMS = (((0,), (0,)), ((), ()))
COLS_DIMS = (((1,), (1,)), ((), ()))


def rms_scale(values):
    return lax.rsqrt(jnp.mean(values * values, axis=-1, keepdims=True) + EPS)


def rms_back(values, gain, upstream):
    factor = rms_scale(values)
    normed = values * factor
    d_normed = upstream * gain
    inner = jnp.mean(d_normed * normed, axis=-1, keepdims=True)
    return (factor * (d_normed - normed * inner), jnp.sum(upstream * normed, axis=0))


def rope_tables(count):
    half_dim = HEAD_DIM // 2
    freqs = THETA ** (-(2.0 * jnp.arange(half_dim).astype(jnp.float32)) / HEAD_DIM)
    places = (jnp.arange(count, dtype=jnp.int32) % SEQ).astype(jnp.float32)
    angles = places[:, None] * freqs[None, :]
    cosine = jnp.concatenate([jnp.cos(angles), jnp.cos(angles)], axis=1)[:, None, :]
    sine = jnp.concatenate([jnp.sin(angles), jnp.sin(angles)], axis=1)[:, None, :]
    return (cosine, sine)


def rotate(values, cosine, sine):
    half_dim = HEAD_DIM // 2
    turned = jnp.concatenate([-values[..., half_dim:], values[..., :half_dim]], axis=-1)
    return values * cosine + turned * sine


def rotate_back(upstream, cosine, sine):
    half_dim = HEAD_DIM // 2
    scaled = upstream * sine
    turned = jnp.concatenate([scaled[..., half_dim:], -scaled[..., :half_dim]], axis=-1)
    return upstream * cosine + turned


def masked_scores(queries, keys_b, seg_groups):
    scores = jnp.einsum("sqhd,skhd->shqk", queries, keys_b, preferred_element_type=jnp.float32)
    scores = scores * HEAD_DIM ** (-0.5)
    index = jnp.arange(SEQ, dtype=jnp.int32)
    causal = index[None, :] <= index[:, None]
    same = seg_groups[:, :, None] == seg_groups[:, None, :]
    allowed = (same & causal[None])[:, None]
    return jnp.where(allowed, scores, -1e30)


def fold_with(activations, incoming):
    return jnp.dot(activations, incoming, preferred_element_type=jnp.float32)


def back_with(upstream, incoming):
    return lax.dot_general(upstream, incoming, COLS_DIMS, preferred_element_type=jnp.float32)


def weight_grad(activations, upstream):
    return lax.psum_scatter(
        lax.dot_general(
            activations, upstream, ROWS_DIMS, preferred_element_type=jnp.float32
        ).astype(jnp.bfloat16),
        "fsdp",
        scatter_dimension=0,
        tiled=True,
    ).astype(jnp.float32)


def gathered(
    tokens,
    segments,
    cotangent,
    qkv_weight,
    out_weight,
    gate_up_weight,
    down_weight,
    q_gain,
    k_gain,
    attn_gain,
    mlp_gain,
):
    count = tokens.shape[0]
    groups = count // SEQ
    qkv = fold_with(tokens, lax.all_gather(qkv_weight, "fsdp", axis=0, tiled=True))
    q_pre, k_pre, v_pre = (qkv[:, :D], qkv[:, D : 2 * D], qkv[:, 2 * D :])
    q_norm = q_pre * rms_scale(q_pre) * q_gain
    k_norm = k_pre * rms_scale(k_pre) * k_gain
    cosine, sine = rope_tables(count)
    q_rot = rotate(q_norm.reshape(count, HEADS, HEAD_DIM), cosine, sine).astype(jnp.bfloat16)
    k_rot = rotate(k_norm.reshape(count, HEADS, HEAD_DIM), cosine, sine).astype(jnp.bfloat16)
    v_b = v_pre.astype(jnp.bfloat16)
    q_grp = q_rot.reshape(groups, SEQ, HEADS, HEAD_DIM)
    k_grp = k_rot.reshape(groups, SEQ, HEADS, HEAD_DIM)
    v_grp = v_b.reshape(groups, SEQ, HEADS, HEAD_DIM)
    seg_groups = segments.reshape(groups, SEQ)
    scores = masked_scores(q_grp, k_grp, seg_groups)
    top = jnp.max(scores, axis=-1, keepdims=True)
    lse = top + jnp.log(jnp.sum(jnp.exp(scores - top), axis=-1, keepdims=True))
    prob_b = jnp.exp(scores - lse).astype(jnp.bfloat16)
    attn = jnp.einsum("shqk,skhd->sqhd", prob_b, v_grp, preferred_element_type=jnp.float32)
    attn_b = attn.reshape(count, D).astype(jnp.bfloat16)
    pre_attn = fold_with(attn_b, lax.all_gather(out_weight, "fsdp", axis=0, tiled=True))
    mid = tokens.astype(jnp.float32) + pre_attn * rms_scale(pre_attn) * attn_gain
    mid_b = mid.astype(jnp.bfloat16)
    gate_up = fold_with(mid_b, lax.all_gather(gate_up_weight, "fsdp", axis=0, tiled=True))
    gate, upper = (gate_up[:, :FF], gate_up[:, FF:])
    sigma = jax.nn.sigmoid(gate)
    hidden_b = (gate * sigma * upper).astype(jnp.bfloat16)
    pre_mlp = fold_with(hidden_b, lax.all_gather(down_weight, "fsdp", axis=0, tiled=True))
    result = (mid + pre_mlp * rms_scale(pre_mlp) * mlp_gain).astype(jnp.bfloat16)
    d_pre_mlp, mlp_gain_part = rms_back(pre_mlp, mlp_gain, cotangent)
    dmlp_b = d_pre_mlp.astype(jnp.bfloat16)
    down_part = weight_grad(hidden_b, dmlp_b)
    d_hidden = back_with(dmlp_b, lax.all_gather(down_weight, "fsdp", axis=0, tiled=True))
    d_gate = d_hidden * upper * sigma * (1.0 + gate * (1.0 - sigma))
    d_upper = d_hidden * gate * sigma
    dgu_b = jnp.concatenate([d_gate, d_upper], axis=1).astype(jnp.bfloat16)
    gate_up_part = weight_grad(mid_b, dgu_b)
    d_mid = cotangent + back_with(dgu_b, lax.all_gather(gate_up_weight, "fsdp", axis=0, tiled=True))
    d_pre_attn, attn_gain_part = rms_back(pre_attn, attn_gain, d_mid)
    dattn_in_b = d_pre_attn.astype(jnp.bfloat16)
    out_part = weight_grad(attn_b, dattn_in_b)
    d_attn_b = back_with(dattn_in_b, lax.all_gather(out_weight, "fsdp", axis=0, tiled=True)).astype(
        jnp.bfloat16
    )
    d_attn_grp = d_attn_b.reshape(groups, SEQ, HEADS, HEAD_DIM)
    prob = jnp.exp(masked_scores(q_grp, k_grp, seg_groups) - lse)
    d_value = jnp.einsum("shqk,sqhd->skhd", prob_b, d_attn_grp, preferred_element_type=jnp.float32)
    d_prob = jnp.einsum("sqhd,skhd->shqk", d_attn_grp, v_grp, preferred_element_type=jnp.float32)
    delta = jnp.sum(prob * d_prob, axis=-1, keepdims=True)
    ds_b = (prob * (d_prob - delta) * HEAD_DIM ** (-0.5)).astype(jnp.bfloat16)
    dq_rot = jnp.einsum("shqk,skhd->sqhd", ds_b, k_grp, preferred_element_type=jnp.float32)
    dk_rot = jnp.einsum("shqk,sqhd->skhd", ds_b, q_grp, preferred_element_type=jnp.float32)
    d_q_norm = rotate_back(dq_rot.reshape(count, HEADS, HEAD_DIM), cosine, sine).reshape(count, D)
    d_k_norm = rotate_back(dk_rot.reshape(count, HEADS, HEAD_DIM), cosine, sine).reshape(count, D)
    d_q_pre, q_gain_part = rms_back(q_pre, q_gain, d_q_norm)
    d_k_pre, k_gain_part = rms_back(k_pre, k_gain, d_k_norm)
    dqkv_b = jnp.concatenate([d_q_pre, d_k_pre, d_value.reshape(count, D)], axis=1).astype(
        jnp.bfloat16
    )
    qkv_part = weight_grad(tokens, dqkv_b)
    input_grad = d_mid + back_with(dqkv_b, lax.all_gather(qkv_weight, "fsdp", axis=0, tiled=True))
    qkv_grad, out_grad, gate_up_grad, down_grad = (
        lax.psum(qkv_part.astype(jnp.bfloat16), "replica").astype(jnp.float32),
        lax.psum(out_part.astype(jnp.bfloat16), "replica").astype(jnp.float32),
        lax.psum(gate_up_part.astype(jnp.bfloat16), "replica").astype(jnp.float32),
        lax.psum(down_part.astype(jnp.bfloat16), "replica").astype(jnp.float32),
    )
    q_gain_grad, k_gain_grad, attn_gain_grad, mlp_gain_grad = lax.psum(
        (q_gain_part, k_gain_part, attn_gain_part, mlp_gain_part), ("replica", "fsdp")
    )
    return (
        result,
        input_grad,
        qkv_grad,
        out_grad,
        gate_up_grad,
        down_grad,
        q_gain_grad,
        k_gain_grad,
        attn_gain_grad,
        mlp_gain_grad,
    )


def swap_pairs(count, bits):
    return [(i, i ^ bits) for i in range(count)]


def lane_pairs(hops):
    return [(2 * a + y, 2 * b + y) for a, b in hops for y in range(2)]


OUTER_IN = ((3, 2), (0, 1))
INNER_OUT = ((2, 3), (1, 0))
MIDDLE = ((1, 2), (2, 1))


def hop(value, bits):
    return lax.ppermute(value, "fsdp", swap_pairs(8, bits))


def lane(value, hops):
    return lax.ppermute(value, "fsdp", lane_pairs(hops))


BF16 = jnp.bfloat16
F32 = jnp.float32


def spread(own, early=None, late=None):
    s1 = hop(own, 1)
    s2 = hop(own, 2)
    near = lane(own, MIDDLE)
    if early is not None:
        s2, near = early(s2, near)
    s3 = hop(s2, 1)
    far = lane(s2, MIDDLE)
    if late is not None:
        far = late(far)
    s4 = far + lane(near, INNER_OUT)
    s5 = hop(s4, 1)
    s6 = near + lane(far, INNER_OUT)
    s7 = hop(s6, 1)
    return [own, s1, s2, s3, s4, s5, s6, s7]


def collect(make):
    narrow = lambda value: value.astype(jnp.bfloat16)
    wide = lambda value: value.astype(jnp.float32)
    held = {}
    for j in (3, 2, 1, 0):
        part = make(j)
        held[j] = part[0] + wide(hop(narrow(part[1]), 1))
    far = held[2] + wide(lane(narrow(held[3]), OUTER_IN))
    near = held[3] + wide(lane(narrow(held[2]), OUTER_IN))
    next_to = held[1] + wide(lane(narrow(far), MIDDLE))
    near_got = wide(lane(narrow(near), MIDDLE))
    return held[0] + near_got + wide(hop(narrow(next_to), 2))


def core_hop(value):
    return lax.ppermute(value, "replica", swap_pairs(4, 1))


def chip_hop(value):
    return lax.ppermute(value, "replica", swap_pairs(4, 2))


def absolute(blocks, index):
    held = jnp.zeros((len(blocks),) + blocks[0].shape, blocks[0].dtype)
    for k, block in enumerate(blocks):
        held = lax.dynamic_update_slice_in_dim(held, block[None], index ^ k, axis=0)
    return held


def swap_blocks(block_for):
    return [block_for(0)] + [hop(block_for(k), k) for k in range(1, 8)]


def replica_gather(block):
    across = chip_hop(block)
    return [block, core_hop(block), across, core_hop(across)]


def call(body, grid, ins, outs, shapes, flops=0, moved=0, scalars=0):
    return pl.pallas_call(
        body,
        grid_spec=pltpu.PrefetchScalarGridSpec(
            num_scalar_prefetch=scalars, grid=grid, in_specs=ins, out_specs=outs
        ),
        out_shape=shapes,
        compiler_params=pltpu.CompilerParams(
            dimension_semantics=("arbitrary",) * len(grid), vmem_limit_bytes=32 * 1024 * 1024
        ),
        cost_estimate=pl.CostEstimate(flops=flops, bytes_accessed=moved, transcendentals=0),
    )


def pair_body(own, got, out):
    for k in range(8):
        out[k] = own[k] + got[k ^ 1]


def sum_body(inverse, *refs):
    out = refs[-1]
    for k in range(8):
        total = refs[0][k]
        for j in range(1, 4):
            total = total + refs[j][k ^ (2 * j)]
        out[k] = total
        out[k, :2] = lax.rsqrt(total[:2] / D + EPS) if inverse else total[:2] / D


def slot_mean(values, inverse):
    spec = pl.BlockSpec(values.shape, lambda i: (0, 0, 0))
    shape = jax.ShapeDtypeStruct(values.shape, F32)
    pair = call(pair_body, (1,), [spec] * 2, spec, shape)(values, hop(values, 1))
    parts = [pair] + [hop(pair, bits) for bits in (2, 4, 6)]
    return call(lambda *refs: sum_body(inverse, *refs), (1,), [spec] * 4, spec, shape)(*parts)


def diagonal():
    down = lax.broadcasted_iota(jnp.int32, (SEQ, SEQ), 0)
    right = lax.broadcasted_iota(jnp.int32, (SEQ, SEQ), 1)
    return down, right


def upright(row):
    down, right = diagonal()
    return jnp.sum(jnp.where(down == right, row, 0.0), axis=1, keepdims=True)


def flat(column):
    down, right = diagonal()
    return jnp.sum(jnp.where(down == right, column, 0.0), axis=0, keepdims=True)


def nt(a, b):
    return lax.dot_general(a, b, COLS_DIMS, preferred_element_type=F32)


def tn(a, b):
    return lax.dot_general(a, b, ROWS_DIMS, preferred_element_type=F32)


def allowed_pairs(fac_ref):
    down, right = diagonal()
    row = fac_ref[0, 2:3, :]
    return (upright(row) == row) & (right <= down)


def softmax(q, k, allowed):
    scores = jnp.where(allowed, nt(q, k) * HEAD_DIM ** (-0.5), -1e30)
    top = jnp.max(scores, axis=1, keepdims=True)
    lse = top + jnp.log(jnp.sum(jnp.exp(scores - top), axis=1, keepdims=True))
    return jnp.exp(scores - lse)


def attend_body(qkv_ref, fac_ref, gain_ref, cos_ref, sin_ref, rot_ref, attn_ref):
    for n in range(fac_ref.shape[0]):
        at = pl.ds(n * SEQ, SEQ)
        one = pl.ds(n, 1)
        attend_one(
            qkv_ref.at[at], fac_ref.at[one], gain_ref, cos_ref, sin_ref, rot_ref.at[at], attn_ref.at[at]
        )


def attend_one(qkv_ref, fac_ref, gain_ref, cos_ref, sin_ref, rot_ref, attn_ref):
    wide = attn_ref.shape[1]
    allowed = allowed_pairs(fac_ref)
    cosine, sine = cos_ref[...], sin_ref[...]
    factor = [upright(fac_ref[0, i : i + 1, :]) for i in range(2)]
    for h in range(wide // HEAD_DIM):
        turned = []
        for i in range(2):
            at = slice(i * wide + h * HEAD_DIM, i * wide + (h + 1) * HEAD_DIM)
            value = qkv_ref[:, at] * factor[i] * gain_ref[i : i + 1, h * HEAD_DIM : (h + 1) * HEAD_DIM]
            value = value * cosine + pltpu.roll(value, HEAD_DIM // 2, 1) * sine
            turned.append(value.astype(BF16))
            rot_ref[:, at] = turned[i]
        at = slice(2 * wide + h * HEAD_DIM, 2 * wide + (h + 1) * HEAD_DIM)
        value_b = qkv_ref[:, at].astype(BF16)
        rot_ref[:, at] = value_b
        prob_b = softmax(turned[0], turned[1], allowed).astype(BF16)
        attn = jnp.dot(prob_b, value_b, preferred_element_type=F32)
        attn_ref[:, h * HEAD_DIM : (h + 1) * HEAD_DIM] = attn.astype(BF16)


def attend_back_body(
    rot_ref, up_ref, qkv_ref, fac_ref, gain_ref, cos_ref, sin_ref, dn_ref, dv_ref, inner_ref, sum_ref
):
    @pl.when(pl.program_id(0) == 0)
    def _():
        sum_ref[...] = jnp.zeros_like(sum_ref)

    for n in range(fac_ref.shape[0]):
        at = pl.ds(n * SEQ, SEQ)
        one = pl.ds(n, 1)
        attend_back_one(
            rot_ref.at[at],
            up_ref.at[at],
            qkv_ref.at[at],
            fac_ref.at[one],
            gain_ref,
            cos_ref,
            sin_ref,
            dn_ref.at[at],
            dv_ref.at[at],
            inner_ref.at[one],
            sum_ref,
        )


def attend_back_one(
    rot_ref, up_ref, qkv_ref, fac_ref, gain_ref, cos_ref, sin_ref, dn_ref, dv_ref, inner_ref, sum_ref
):
    wide = up_ref.shape[1]
    allowed = allowed_pairs(fac_ref)
    cosine, sine = cos_ref[...], sin_ref[...]
    factor = [upright(fac_ref[0, i : i + 1, :]) for i in range(2)]
    inner = [0.0, 0.0]
    for h in range(wide // HEAD_DIM):
        own = slice(h * HEAD_DIM, (h + 1) * HEAD_DIM)
        q, k, v = (
            rot_ref[:, i * wide + h * HEAD_DIM : i * wide + (h + 1) * HEAD_DIM] for i in range(3)
        )
        up = up_ref[:, own]
        prob = softmax(q, k, allowed)
        dv_ref[:, own] = tn(prob.astype(BF16), up).astype(BF16)
        d_prob = nt(up, v)
        delta = jnp.sum(prob * d_prob, axis=1, keepdims=True)
        ds_b = (prob * (d_prob - delta) * HEAD_DIM ** (-0.5)).astype(BF16)
        back = (jnp.dot(ds_b, k, preferred_element_type=F32), tn(ds_b, q))
        for i in range(2):
            at = slice(i * wide + h * HEAD_DIM, i * wide + (h + 1) * HEAD_DIM)
            d_norm = back[i] * cosine + pltpu.roll(back[i] * sine, HEAD_DIM // 2, 1)
            dn_ref[:, at] = d_norm
            unit = qkv_ref[:, at] * factor[i]
            inner[i] = inner[i] + jnp.sum(
                d_norm * gain_ref[i : i + 1, own] * unit, axis=1, keepdims=True
            )
            sum_ref[i : i + 1, own] += jnp.sum(d_norm * unit, axis=0, keepdims=True)
    for i in range(2):
        inner_ref[0, i : i + 1, :] = flat(inner[i])


def norm_back_body(dn_ref, dv_ref, qkv_ref, fac_ref, mean_ref, gain_ref, out_ref):
    wide = dv_ref.shape[1]
    for i in range(2):
        at = slice(i * wide, (i + 1) * wide)
        factor = upright(fac_ref[0, i : i + 1, :])
        mean = upright(mean_ref[0, i : i + 1, :])
        unit = qkv_ref[:, at] * factor
        value = factor * (dn_ref[:, at] * gain_ref[i : i + 1, :] - unit * mean)
        out_ref[:, at] = value.astype(BF16)
    out_ref[:, 2 * wide :] = dv_ref[...]


def gate_up_body(copy_ref, *refs):
    out = refs[-1]
    width = refs[0].shape[2]
    for m in range(4):
        start = pl.multiple_of((copy_ref[0] ^ m) * width, width)
        out[:, pl.ds(start, width)] = refs[m][0].astype(F32)


def qkv_body(copy_ref, *refs):
    out = refs[-1]
    members, height, width = refs[0].shape
    for m in range(4):
        start = pl.multiple_of((copy_ref[0] ^ m) * height, height)
        for i in range(members):
            out[pl.ds(start, height), i * width : (i + 1) * width] = refs[m][i].astype(F32)


def halves(left, right, core, height):
    own = lax.dynamic_slice_in_dim(left, core * height, height, axis=1)
    other = lax.dynamic_slice_in_dim(left, (1 - core) * height, height, axis=1)
    return (tn(own, right) + core_hop(tn(other, right).astype(BF16)).astype(F32)).astype(BF16)


def join_halves(pair_b, other, core):
    total = (pair_b.astype(F32) + other.astype(F32)).astype(BF16)
    back = core_hop(total)
    first = jnp.where(core == 0, total, back)
    second = jnp.where(core == 0, back, total)
    return jnp.concatenate([first, second]).astype(F32)


tie = lax.optimization_barrier


def tensor_split(
    tokens,
    segments,
    cotangent,
    qkv_weight,
    out_weight,
    gate_up_weight,
    down_weight,
    q_gain,
    k_gain,
    attn_gain,
    mlp_gain,
):
    members, copies = 8, 4
    rows = tokens.shape[0]
    count = members * rows
    wide = D // members
    units = FF // members
    quarter = units // copies
    place = lax.axis_index("fsdp")
    copy = lax.axis_index("replica")
    core = copy % 2
    owned = qkv_weight.shape[0]
    sub = owned // copies
    copy_at = copy.astype(jnp.int32).reshape(1)

    def qkv_block(k):
        parts = [
            lax.dynamic_slice(qkv_weight, (copy * sub, i * D + (place ^ k) * wide), (sub, wide))
            for i in range(3)
        ]
        return jnp.concatenate(parts, axis=1)

    def gate_up_block(member):
        parts = [
            lax.dynamic_slice_in_dim(
                gate_up_source, i * FF + member * units + copy * quarter, quarter, axis=1
            )
            for i in range(2)
        ]
        return jnp.concatenate(parts, axis=1)

    mine = lambda gain: lax.dynamic_slice_in_dim(gain, place * wide, wide)
    gain_own = jnp.stack([mine(q_gain), mine(k_gain)])

    qkv_blocks = swap_blocks(qkv_block)
    gate_up_source = gate_up_weight

    def early(s2, near):
        nonlocal gate_up_source
        s2, near, gate_up_source = tie((s2, near, gate_up_weight))
        return s2, near

    def late(far):
        nonlocal qkv_blocks
        far, qkv_blocks = tie((far, qkv_blocks))
        return far

    token_slots = spread(tokens, early, late)
    pieces = absolute(replica_gather(absolute(qkv_blocks, place)), copy)
    qkv_cols = pieces.transpose(1, 0, 2, 3).reshape(D, 3 * wide)
    cosine, sine = rope_tables(rows)
    sign = jnp.where(jnp.arange(HEAD_DIM) < HEAD_DIM // 2, -1.0, 1.0)
    cosine, sine = cosine[:, 0], sine[:, 0] * sign

    token_all = jnp.concatenate(token_slots)
    qkv = fold_with(token_all, qkv_cols)
    gate_up_piece = jnp.stack([gate_up_block(i) for i in range(members)])
    gate_up_piece = lax.all_to_all(gate_up_piece, "fsdp", 0, 0, tiled=True).reshape(D, 2 * quarter)

    q_pre, k_pre = (qkv[:, :wide], qkv[:, wide : 2 * wide])
    squares = [jnp.sum(value * value, axis=1).reshape(members, rows) for value in (q_pre, k_pre)]
    seg_rows = jnp.zeros((members, rows), F32).at[0].set(segments.astype(F32))
    factors = slot_mean(jnp.stack(squares + [seg_rows], axis=1), True)
    slab = lambda width, n=1: pl.BlockSpec((n * rows, width), lambda i: (i, 0))
    line = lambda height, n=1: pl.BlockSpec((n, height, rows), lambda i: (i, 0, 0))
    whole = lambda shape: pl.BlockSpec(shape, lambda i: (0,) * len(shape))
    tables = [whole((2, wide)), whole((rows, HEAD_DIM)), whole((rows, HEAD_DIM))]
    rot, attn_b = call(
        attend_body,
        (members // 2,),
        [slab(3 * wide, 2), line(3, 2)] + tables,
        [slab(3 * wide, 2), slab(wide, 2)],
        [jax.ShapeDtypeStruct((count, 3 * wide), BF16), jax.ShapeDtypeStruct((count, wide), BF16)],
        flops=4 * count * rows * wide,
        moved=count * wide * 20,
    )(qkv, factors, gain_own, cosine, sine)

    span = 2 * rows
    rows_of = lambda value, j: value[j * span : (j + 1) * span]
    pre_attn = collect(lambda j: fold_with(rows_of(attn_b, j), out_weight).reshape(2, rows, D))
    gate_up_all = replica_gather(gate_up_piece)
    mid = tokens.astype(F32) + pre_attn * rms_scale(pre_attn) * attn_gain
    mid_b = mid.astype(BF16)

    def late_mid(far):
        nonlocal gate_up_all
        far, gate_up_all = tie((far, gate_up_all))
        return far

    mid_all = jnp.concatenate(spread(mid_b, None, late_mid))
    gate_up_cols = absolute(gate_up_all, copy)
    gate_up = [fold_with(mid_all, gate_up_cols[c]) for c in range(copies)]
    gate = [value[:, :quarter] for value in gate_up]
    upper = [value[:, quarter:] for value in gate_up]
    sigma = [jax.nn.sigmoid(value) for value in gate]
    hidden_b = jnp.concatenate(
        [(g * s * u).astype(BF16) for g, s, u in zip(gate, sigma, upper)], axis=1
    )
    pre_mlp = collect(lambda j: fold_with(rows_of(hidden_b, j), down_weight).reshape(2, rows, D))
    result = (mid + pre_mlp * rms_scale(pre_mlp) * mlp_gain).astype(BF16)
    d_pre_mlp, mlp_gain_part = rms_back(pre_mlp, mlp_gain, cotangent)
    dmlp_b = d_pre_mlp.astype(BF16)

    dmlp_all = jnp.concatenate(spread(dmlp_b))
    d_hidden = back_with(dmlp_all, down_weight)
    dgu = []
    for c in range(copies):
        d_h = d_hidden[:, c * quarter : (c + 1) * quarter]
        d_gate = d_h * upper[c] * sigma[c] * (1.0 + gate[c] * (1.0 - sigma[c]))
        d_upper = d_h * gate[c] * sigma[c]
        dgu.append(jnp.concatenate([d_gate, d_upper], axis=1).astype(BF16))

    def d_mid_part(j):
        total = back_with(rows_of(dgu[0], j), gate_up_cols[0])
        for c in range(1, copies):
            total = total + back_with(rows_of(dgu[c], j), gate_up_cols[c])
        return total.reshape(2, rows, D)

    dgu_all = jnp.stack(dgu)
    quarter_grad = lambda m: tn(
        mid_all, lax.dynamic_index_in_dim(dgu_all, copy ^ m, axis=0, keepdims=False)
    )
    kept = {}

    def d_mid_step(j):
        if j == 1:
            pair = halves(hidden_b, dmlp_all, core, units // 2)
            dgu[0], kept["pair"] = tie((dgu[0], pair))
            kept["down"] = chip_hop(kept["pair"])
        if j == 0:
            sends = [quarter_grad(m).astype(BF16) for m in (3, 1)]
            dgu[0], *sends = tie((dgu[0], *sends))
            kept[3], kept[1] = (core_hop(value) for value in sends)
            sent = (quarter_grad(2) + kept[3].astype(F32)).astype(BF16)
            kept[2] = chip_hop(sent)
            kept[0] = quarter_grad(0) + kept[1].astype(F32)
        return d_mid_part(j)

    d_mid = cotangent + collect(d_mid_step)
    d_mid, gate_up_own = tie((d_mid, kept[0]))
    down_pair, down_other = kept["pair"], kept["down"]
    gate_up_part = (gate_up_own + kept[2].astype(F32)).astype(BF16)

    d_pre_attn, attn_gain_part = rms_back(pre_attn, attn_gain, d_mid)
    dattn_all = jnp.concatenate(spread(d_pre_attn.astype(BF16)))
    dattn_all, gate_up_part = tie((dattn_all, gate_up_part))
    d_attn_b = back_with(dattn_all, out_weight).astype(BF16)
    gate_up_part = gate_up_part.reshape(members, owned, 2 * quarter)
    gate_up_part = lax.all_to_all(gate_up_part, "fsdp", 0, 0, tiled=True)
    attend_back = call(
        attend_back_body,
        (members // 2,),
        [slab(3 * wide, 2), slab(wide, 2), slab(3 * wide, 2), line(3, 2)] + tables,
        [slab(2 * wide, 2), slab(wide, 2), line(2, 2), whole((2, wide))],
        [
            jax.ShapeDtypeStruct((count, 2 * wide), F32),
            jax.ShapeDtypeStruct((count, wide), BF16),
            jax.ShapeDtypeStruct((members, 2, rows), F32),
            jax.ShapeDtypeStruct((2, wide), F32),
        ],
        flops=10 * count * rows * wide,
        moved=count * wide * 30,
    )
    d_norm, d_value, inner, gain_sums = attend_back(rot, d_attn_b, qkv, factors, gain_own, cosine, sine)
    inner, dattn_late = tie((inner, dattn_all))
    means = slot_mean(inner, False)
    means, down_pair = tie((means, down_pair))
    out_pair = halves(attn_b, dattn_late, core, wide // 2)
    out_other = chip_hop(out_pair)
    dqkv_b = call(
        norm_back_body,
        (members,),
        [slab(2 * wide), slab(wide), slab(3 * wide), line(3), line(2), whole((2, wide))],
        slab(3 * wide),
        jax.ShapeDtypeStruct((count, 3 * wide), BF16),
        flops=count * wide * 10,
        moved=count * wide * 28,
    )(d_norm, d_value, qkv, factors, means, gain_own)
    blank = jnp.zeros((2, D), F32)
    gains = jnp.concatenate(
        [
            lax.dynamic_update_slice_in_dim(blank, gain_sums, place * wide, axis=1),
            attn_gain_part[None],
            mlp_gain_part[None],
        ]
    )
    gains = gains + chip_hop(gains)
    gains = gains + core_hop(gains)
    for bits in (1, 2, 4):
        gains = gains + hop(gains, bits)
    down_grad = join_halves(down_pair, down_other, core)
    dqkv_b, out_other = tie((dqkv_b, out_other))

    qkv_full = tn(token_all, dqkv_b).reshape(members, copies, sub, 3 * wide)
    part_for = lambda m: lax.dynamic_index_in_dim(qkv_full, copy ^ m, axis=1, keepdims=False)
    third, first = part_for(3).astype(BF16), part_for(1).astype(BF16)
    dqkv_b, third, first = tie((dqkv_b, third, first))
    qkv_sent = (part_for(2) + core_hop(third).astype(F32)).astype(BF16)
    qkv_own = part_for(0) + core_hop(first).astype(F32)
    qkv_part = (qkv_own + chip_hop(qkv_sent).astype(F32)).astype(BF16)
    gate_up_parts = replica_gather(gate_up_part)
    qkv_blocks = swap_blocks(
        lambda k: lax.dynamic_index_in_dim(qkv_part, place ^ k, axis=0, keepdims=False)
    )
    input_grad = d_mid + collect(
        lambda j: back_with(rows_of(dqkv_b, j), qkv_cols).reshape(2, rows, D)
    )
    out_grad = join_halves(out_pair, out_other, core)
    gate_up_grad = call(
        gate_up_body,
        (2, members),
        [pl.BlockSpec((1, owned, quarter), lambda h, i, c: (i, 0, h))] * copies,
        pl.BlockSpec((owned, units), lambda h, i, c: (0, h * members + i)),
        jax.ShapeDtypeStruct((owned, 2 * FF), F32),
        moved=owned * FF * 12,
        scalars=1,
    )(copy_at, *gate_up_parts)
    qkv_blocks, out_grad, gains = tie((qkv_blocks, out_grad, gains))
    qkv_grad = call(
        qkv_body,
        (3,),
        [pl.BlockSpec((members, sub, wide), lambda i, c: (0, 0, i))] * copies,
        pl.BlockSpec((owned, D), lambda i, c: (0, i)),
        jax.ShapeDtypeStruct((owned, 3 * D), F32),
        moved=owned * D * 18,
        scalars=1,
    )(copy_at, *replica_gather(absolute(qkv_blocks, place)))
    return (
        result,
        input_grad,
        qkv_grad,
        out_grad,
        gate_up_grad,
        down_grad,
        gains[0],
        gains[1],
        gains[2],
        gains[3],
    )


def solution(mesh):
    def per_device(*arrays):
        fits = mesh.shape["fsdp"] == 8 and mesh.shape["replica"] == 4 and arrays[0].shape[0] == SEQ
        if not fits:
            return gathered(*arrays)
        return tensor_split(*arrays)


    placed = (
        P(("replica", "fsdp"), None),
        P(("replica", "fsdp")),
        P(("replica", "fsdp"), None),
        P("fsdp", None),
        P("fsdp", None),
        P("fsdp", None),
        P("fsdp", None),
        P(),
        P(),
        P(),
        P(),
    )
    return jax.shard_map(
        per_device,
        mesh=mesh,
        in_specs=placed,
        out_specs=(
            P(("replica", "fsdp"), None),
            P(("replica", "fsdp"), None),
            P("fsdp", None),
            P("fsdp", None),
            P("fsdp", None),
            P("fsdp", None),
            P(),
            P(),
            P(),
            P(),
        ),
        check_vma=False,
    )
```

```python
import jax
import jax.numpy as jnp
from jax import lax
from jax.experimental import pallas as pl
from jax.experimental.pallas import tpu as pltpu
from jax.sharding import PartitionSpec as P


D = 2048
HEADS = 16
HEAD_DIM = 128
FF = 8192
SEQ = 128


EPS = 1e-06
THETA = 500000.0
ROWS_DIMS = (((0,), (0,)), ((), ()))
COLS_DIMS = (((1,), (1,)), ((), ()))


def rms_scale(values):
    return lax.rsqrt(jnp.mean(values * values, axis=-1, keepdims=True) + EPS)


def rms_back(values, gain, upstream):
    factor = rms_scale(values)
    normed = values * factor
    d_normed = upstream * gain
    inner = jnp.mean(d_normed * normed, axis=-1, keepdims=True)
    return (factor * (d_normed - normed * inner), jnp.sum(upstream * normed, axis=0))


def rope_tables(count):
    half_dim = HEAD_DIM // 2
    freqs = THETA ** (-(2.0 * jnp.arange(half_dim).astype(jnp.float32)) / HEAD_DIM)
    places = (jnp.arange(count, dtype=jnp.int32) % SEQ).astype(jnp.float32)
    angles = places[:, None] * freqs[None, :]
    cosine = jnp.concatenate([jnp.cos(angles), jnp.cos(angles)], axis=1)[:, None, :]
    sine = jnp.concatenate([jnp.sin(angles), jnp.sin(angles)], axis=1)[:, None, :]
    return (cosine, sine)


def rotate(values, cosine, sine):
    half_dim = HEAD_DIM // 2
    turned = jnp.concatenate([-values[..., half_dim:], values[..., :half_dim]], axis=-1)
    return values * cosine + turned * sine


def rotate_back(upstream, cosine, sine):
    half_dim = HEAD_DIM // 2
    scaled = upstream * sine
    turned = jnp.concatenate([scaled[..., half_dim:], -scaled[..., :half_dim]], axis=-1)
    return upstream * cosine + turned


def masked_scores(queries, keys_b, seg_groups):
    scores = jnp.einsum("sqhd,skhd->shqk", queries, keys_b, preferred_element_type=jnp.float32)
    scores = scores * HEAD_DIM ** (-0.5)
    index = jnp.arange(SEQ, dtype=jnp.int32)
    causal = index[None, :] <= index[:, None]
    same = seg_groups[:, :, None] == seg_groups[:, None, :]
    allowed = (same & causal[None])[:, None]
    return jnp.where(allowed, scores, -1e30)


def fold_with(activations, incoming):
    return jnp.dot(activations, incoming, preferred_element_type=jnp.float32)


def back_with(upstream, incoming):
    return lax.dot_general(upstream, incoming, COLS_DIMS, preferred_element_type=jnp.float32)


def weight_grad(activations, upstream):
    return lax.psum_scatter(
        lax.dot_general(
            activations, upstream, ROWS_DIMS, preferred_element_type=jnp.float32
        ).astype(jnp.bfloat16),
        "fsdp",
        scatter_dimension=0,
        tiled=True,
    ).astype(jnp.float32)


def gathered(
    tokens,
    segments,
    cotangent,
    qkv_weight,
    out_weight,
    gate_up_weight,
    down_weight,
    q_gain,
    k_gain,
    attn_gain,
    mlp_gain,
):
    count = tokens.shape[0]
    groups = count // SEQ
    qkv = fold_with(tokens, lax.all_gather(qkv_weight, "fsdp", axis=0, tiled=True))
    q_pre, k_pre, v_pre = (qkv[:, :D], qkv[:, D : 2 * D], qkv[:, 2 * D :])
    q_norm = q_pre * rms_scale(q_pre) * q_gain
    k_norm = k_pre * rms_scale(k_pre) * k_gain
    cosine, sine = rope_tables(count)
    q_rot = rotate(q_norm.reshape(count, HEADS, HEAD_DIM), cosine, sine).astype(jnp.bfloat16)
    k_rot = rotate(k_norm.reshape(count, HEADS, HEAD_DIM), cosine, sine).astype(jnp.bfloat16)
    v_b = v_pre.astype(jnp.bfloat16)
    q_grp = q_rot.reshape(groups, SEQ, HEADS, HEAD_DIM)
    k_grp = k_rot.reshape(groups, SEQ, HEADS, HEAD_DIM)
    v_grp = v_b.reshape(groups, SEQ, HEADS, HEAD_DIM)
    seg_groups = segments.reshape(groups, SEQ)
    scores = masked_scores(q_grp, k_grp, seg_groups)
    top = jnp.max(scores, axis=-1, keepdims=True)
    lse = top + jnp.log(jnp.sum(jnp.exp(scores - top), axis=-1, keepdims=True))
    prob_b = jnp.exp(scores - lse).astype(jnp.bfloat16)
    attn = jnp.einsum("shqk,skhd->sqhd", prob_b, v_grp, preferred_element_type=jnp.float32)
    attn_b = attn.reshape(count, D).astype(jnp.bfloat16)
    pre_attn = fold_with(attn_b, lax.all_gather(out_weight, "fsdp", axis=0, tiled=True))
    mid = tokens.astype(jnp.float32) + pre_attn * rms_scale(pre_attn) * attn_gain
    mid_b = mid.astype(jnp.bfloat16)
    gate_up = fold_with(mid_b, lax.all_gather(gate_up_weight, "fsdp", axis=0, tiled=True))
    gate, upper = (gate_up[:, :FF], gate_up[:, FF:])
    sigma = jax.nn.sigmoid(gate)
    hidden_b = (gate * sigma * upper).astype(jnp.bfloat16)
    pre_mlp = fold_with(hidden_b, lax.all_gather(down_weight, "fsdp", axis=0, tiled=True))
    result = (mid + pre_mlp * rms_scale(pre_mlp) * mlp_gain).astype(jnp.bfloat16)
    d_pre_mlp, mlp_gain_part = rms_back(pre_mlp, mlp_gain, cotangent)
    dmlp_b = d_pre_mlp.astype(jnp.bfloat16)
    down_part = weight_grad(hidden_b, dmlp_b)
    d_hidden = back_with(dmlp_b, lax.all_gather(down_weight, "fsdp", axis=0, tiled=True))
    d_gate = d_hidden * upper * sigma * (1.0 + gate * (1.0 - sigma))
    d_upper = d_hidden * gate * sigma
    dgu_b = jnp.concatenate([d_gate, d_upper], axis=1).astype(jnp.bfloat16)
    gate_up_part = weight_grad(mid_b, dgu_b)
    d_mid = cotangent + back_with(dgu_b, lax.all_gather(gate_up_weight, "fsdp", axis=0, tiled=True))
    d_pre_attn, attn_gain_part = rms_back(pre_attn, attn_gain, d_mid)
    dattn_in_b = d_pre_attn.astype(jnp.bfloat16)
    out_part = weight_grad(attn_b, dattn_in_b)
    d_attn_b = back_with(dattn_in_b, lax.all_gather(out_weight, "fsdp", axis=0, tiled=True)).astype(
        jnp.bfloat16
    )
    d_attn_grp = d_attn_b.reshape(groups, SEQ, HEADS, HEAD_DIM)
    prob = jnp.exp(masked_scores(q_grp, k_grp, seg_groups) - lse)
    d_value = jnp.einsum("shqk,sqhd->skhd", prob_b, d_attn_grp, preferred_element_type=jnp.float32)
    d_prob = jnp.einsum("sqhd,skhd->shqk", d_attn_grp, v_grp, preferred_element_type=jnp.float32)
    delta = jnp.sum(prob * d_prob, axis=-1, keepdims=True)
    ds_b = (prob * (d_prob - delta) * HEAD_DIM ** (-0.5)).astype(jnp.bfloat16)
    dq_rot = jnp.einsum("shqk,skhd->sqhd", ds_b, k_grp, preferred_element_type=jnp.float32)
    dk_rot = jnp.einsum("shqk,sqhd->skhd", ds_b, q_grp, preferred_element_type=jnp.float32)
    d_q_norm = rotate_back(dq_rot.reshape(count, HEADS, HEAD_DIM), cosine, sine).reshape(count, D)
    d_k_norm = rotate_back(dk_rot.reshape(count, HEADS, HEAD_DIM), cosine, sine).reshape(count, D)
    d_q_pre, q_gain_part = rms_back(q_pre, q_gain, d_q_norm)
    d_k_pre, k_gain_part = rms_back(k_pre, k_gain, d_k_norm)
    dqkv_b = jnp.concatenate([d_q_pre, d_k_pre, d_value.reshape(count, D)], axis=1).astype(
        jnp.bfloat16
    )
    qkv_part = weight_grad(tokens, dqkv_b)
    input_grad = d_mid + back_with(dqkv_b, lax.all_gather(qkv_weight, "fsdp", axis=0, tiled=True))
    qkv_grad, out_grad, gate_up_grad, down_grad = (
        lax.psum(qkv_part.astype(jnp.bfloat16), "replica").astype(jnp.float32),
        lax.psum(out_part.astype(jnp.bfloat16), "replica").astype(jnp.float32),
        lax.psum(gate_up_part.astype(jnp.bfloat16), "replica").astype(jnp.float32),
        lax.psum(down_part.astype(jnp.bfloat16), "replica").astype(jnp.float32),
    )
    q_gain_grad, k_gain_grad, attn_gain_grad, mlp_gain_grad = lax.psum(
        (q_gain_part, k_gain_part, attn_gain_part, mlp_gain_part), ("replica", "fsdp")
    )
    return (
        result,
        input_grad,
        qkv_grad,
        out_grad,
        gate_up_grad,
        down_grad,
        q_gain_grad,
        k_gain_grad,
        attn_gain_grad,
        mlp_gain_grad,
    )


def swap_pairs(count, bits):
    return [(i, i ^ bits) for i in range(count)]


def lane_pairs(hops):
    return [(2 * a + y, 2 * b + y) for a, b in hops for y in range(2)]


OUTER_IN = ((3, 2), (0, 1))
INNER_OUT = ((2, 3), (1, 0))
MIDDLE = ((1, 2), (2, 1))


def hop(value, bits):
    return lax.ppermute(value, "fsdp", swap_pairs(8, bits))


def lane(value, hops):
    return lax.ppermute(value, "fsdp", lane_pairs(hops))


BF16 = jnp.bfloat16
F32 = jnp.float32


def spread(own, early=None, late=None):
    s1 = hop(own, 1)
    s2 = hop(own, 2)
    near = lane(own, MIDDLE)
    if early is not None:
        s2, near = early(s2, near)
    s3 = hop(s2, 1)
    far = lane(s2, MIDDLE)
    if late is not None:
        far = late(far)
    s4 = far + lane(near, INNER_OUT)
    s5 = hop(s4, 1)
    s6 = near + lane(far, INNER_OUT)
    s7 = hop(s6, 1)
    return [own, s1, s2, s3, s4, s5, s6, s7]


def collect(make):
    narrow = lambda value: value.astype(jnp.bfloat16)
    wide = lambda value: value.astype(jnp.float32)
    held = {}
    for j in (3, 2, 1, 0):
        part = make(j)
        held[j] = part[0] + wide(hop(narrow(part[1]), 1))
    far = held[2] + wide(lane(narrow(held[3]), OUTER_IN))
    near = held[3] + wide(lane(narrow(held[2]), OUTER_IN))
    next_to = held[1] + wide(lane(narrow(far), MIDDLE))
    near_got = wide(lane(narrow(near), MIDDLE))
    return held[0] + near_got + wide(hop(narrow(next_to), 2))


def core_hop(value):
    return lax.ppermute(value, "replica", swap_pairs(4, 1))


def chip_hop(value):
    return lax.ppermute(value, "replica", swap_pairs(4, 2))


def absolute(blocks, index):
    held = jnp.zeros((len(blocks),) + blocks[0].shape, blocks[0].dtype)
    for k, block in enumerate(blocks):
        held = lax.dynamic_update_slice_in_dim(held, block[None], index ^ k, axis=0)
    return held


def swap_blocks(block_for):
    return [block_for(0)] + [hop(block_for(k), k) for k in range(1, 8)]


def replica_gather(block):
    across = chip_hop(block)
    return [block, core_hop(block), across, core_hop(across)]


def call(body, grid, ins, outs, shapes, flops=0, moved=0, scalars=0):
    return pl.pallas_call(
        body,
        grid_spec=pltpu.PrefetchScalarGridSpec(
            num_scalar_prefetch=scalars, grid=grid, in_specs=ins, out_specs=outs
        ),
        out_shape=shapes,
        compiler_params=pltpu.CompilerParams(
            dimension_semantics=("arbitrary",) * len(grid), vmem_limit_bytes=32 * 1024 * 1024
        ),
        cost_estimate=pl.CostEstimate(flops=flops, bytes_accessed=moved, transcendentals=0),
    )


def pair_body(own, got, out):
    for k in range(8):
        out[k] = own[k] + got[k ^ 1]


def sum_body(inverse, *refs):
    out = refs[-1]
    for k in range(8):
        total = refs[0][k]
        for j in range(1, 4):
            total = total + refs[j][k ^ (2 * j)]
        out[k] = total
        out[k, :2] = lax.rsqrt(total[:2] / D + EPS) if inverse else total[:2] / D


def slot_mean(values, inverse):
    spec = pl.BlockSpec(values.shape, lambda i: (0, 0, 0))
    shape = jax.ShapeDtypeStruct(values.shape, F32)
    pair = call(pair_body, (1,), [spec] * 2, spec, shape)(values, hop(values, 1))
    parts = [pair] + [hop(pair, bits) for bits in (2, 4, 6)]
    return call(lambda *refs: sum_body(inverse, *refs), (1,), [spec] * 4, spec, shape)(*parts)


def diagonal():
    down = lax.broadcasted_iota(jnp.int32, (SEQ, SEQ), 0)
    right = lax.broadcasted_iota(jnp.int32, (SEQ, SEQ), 1)
    return down, right


def upright(row):
    down, right = diagonal()
    return jnp.sum(jnp.where(down == right, row, 0.0), axis=1, keepdims=True)


def flat(column):
    down, right = diagonal()
    return jnp.sum(jnp.where(down == right, column, 0.0), axis=0, keepdims=True)


def nt(a, b):
    return lax.dot_general(a, b, COLS_DIMS, preferred_element_type=F32)


def tn(a, b):
    return lax.dot_general(a, b, ROWS_DIMS, preferred_element_type=F32)


def allowed_pairs(fac_ref):
    down, right = diagonal()
    row = fac_ref[0, 2:3, :]
    return (upright(row) == row) & (right <= down)


def softmax(q, k, allowed):
    scores = jnp.where(allowed, nt(q, k) * HEAD_DIM ** (-0.5), -1e30)
    top = jnp.max(scores, axis=1, keepdims=True)
    lse = top + jnp.log(jnp.sum(jnp.exp(scores - top), axis=1, keepdims=True))
    return jnp.exp(scores - lse)


def attend_body(qkv_ref, fac_ref, gain_ref, cos_ref, sin_ref, rot_ref, attn_ref):
    for n in range(fac_ref.shape[0]):
        at = pl.ds(n * SEQ, SEQ)
        one = pl.ds(n, 1)
        attend_one(
            qkv_ref.at[at], fac_ref.at[one], gain_ref, cos_ref, sin_ref, rot_ref.at[at], attn_ref.at[at]
        )


def attend_one(qkv_ref, fac_ref, gain_ref, cos_ref, sin_ref, rot_ref, attn_ref):
    wide = attn_ref.shape[1]
    allowed = allowed_pairs(fac_ref)
    cosine, sine = cos_ref[...], sin_ref[...]
    factor = [upright(fac_ref[0, i : i + 1, :]) for i in range(2)]
    for h in range(wide // HEAD_DIM):
        turned = []
        for i in range(2):
            at = slice(i * wide + h * HEAD_DIM, i * wide + (h + 1) * HEAD_DIM)
            value = qkv_ref[:, at] * factor[i] * gain_ref[i : i + 1, h * HEAD_DIM : (h + 1) * HEAD_DIM]
            value = value * cosine + pltpu.roll(value, HEAD_DIM // 2, 1) * sine
            turned.append(value.astype(BF16))
            rot_ref[:, at] = turned[i]
        at = slice(2 * wide + h * HEAD_DIM, 2 * wide + (h + 1) * HEAD_DIM)
        value_b = qkv_ref[:, at].astype(BF16)
        rot_ref[:, at] = value_b
        prob_b = softmax(turned[0], turned[1], allowed).astype(BF16)
        attn = jnp.dot(prob_b, value_b, preferred_element_type=F32)
        attn_ref[:, h * HEAD_DIM : (h + 1) * HEAD_DIM] = attn.astype(BF16)


def attend_back_body(
    rot_ref, up_ref, qkv_ref, fac_ref, gain_ref, cos_ref, sin_ref, dn_ref, dv_ref, inner_ref, sum_ref
):
    @pl.when(pl.program_id(0) == 0)
    def _():
        sum_ref[...] = jnp.zeros_like(sum_ref)

    for n in range(fac_ref.shape[0]):
        at = pl.ds(n * SEQ, SEQ)
        one = pl.ds(n, 1)
        attend_back_one(
            rot_ref.at[at],
            up_ref.at[at],
            qkv_ref.at[at],
            fac_ref.at[one],
            gain_ref,
            cos_ref,
            sin_ref,
            dn_ref.at[at],
            dv_ref.at[at],
            inner_ref.at[one],
            sum_ref,
        )


def attend_back_one(
    rot_ref, up_ref, qkv_ref, fac_ref, gain_ref, cos_ref, sin_ref, dn_ref, dv_ref, inner_ref, sum_ref
):
    wide = up_ref.shape[1]
    allowed = allowed_pairs(fac_ref)
    cosine, sine = cos_ref[...], sin_ref[...]
    factor = [upright(fac_ref[0, i : i + 1, :]) for i in range(2)]
    inner = [0.0, 0.0]
    for h in range(wide // HEAD_DIM):
        own = slice(h * HEAD_DIM, (h + 1) * HEAD_DIM)
        q, k, v = (
            rot_ref[:, i * wide + h * HEAD_DIM : i * wide + (h + 1) * HEAD_DIM] for i in range(3)
        )
        up = up_ref[:, own]
        prob = softmax(q, k, allowed)
        dv_ref[:, own] = tn(prob.astype(BF16), up).astype(BF16)
        d_prob = nt(up, v)
        delta = jnp.sum(prob * d_prob, axis=1, keepdims=True)
        ds_b = (prob * (d_prob - delta) * HEAD_DIM ** (-0.5)).astype(BF16)
        back = (jnp.dot(ds_b, k, preferred_element_type=F32), tn(ds_b, q))
        for i in range(2):
            at = slice(i * wide + h * HEAD_DIM, i * wide + (h + 1) * HEAD_DIM)
            d_norm = back[i] * cosine + pltpu.roll(back[i] * sine, HEAD_DIM // 2, 1)
            dn_ref[:, at] = d_norm
            unit = qkv_ref[:, at] * factor[i]
            inner[i] = inner[i] + jnp.sum(
                d_norm * gain_ref[i : i + 1, own] * unit, axis=1, keepdims=True
            )
            sum_ref[i : i + 1, own] += jnp.sum(d_norm * unit, axis=0, keepdims=True)
    for i in range(2):
        inner_ref[0, i : i + 1, :] = flat(inner[i])


def norm_back_body(dn_ref, dv_ref, qkv_ref, fac_ref, mean_ref, gain_ref, out_ref):
    wide = dv_ref.shape[1]
    for i in range(2):
        at = slice(i * wide, (i + 1) * wide)
        factor = upright(fac_ref[0, i : i + 1, :])
        mean = upright(mean_ref[0, i : i + 1, :])
        unit = qkv_ref[:, at] * factor
        value = factor * (dn_ref[:, at] * gain_ref[i : i + 1, :] - unit * mean)
        out_ref[:, at] = value.astype(BF16)
    out_ref[:, 2 * wide :] = dv_ref[...]


def gate_up_body(copy_ref, *refs):
    out = refs[-1]
    width = refs[0].shape[2]
    for m in range(4):
        start = pl.multiple_of((copy_ref[0] ^ m) * width, width)
        out[:, pl.ds(start, width)] = refs[m][0].astype(F32)


def qkv_body(copy_ref, *refs):
    out = refs[-1]
    members, height, width = refs[0].shape
    for m in range(4):
        start = pl.multiple_of((copy_ref[0] ^ m) * height, height)
        for i in range(members):
            out[pl.ds(start, height), i * width : (i + 1) * width] = refs[m][i].astype(F32)


def halves(left, right, core, height):
    own = lax.dynamic_slice_in_dim(left, core * height, height, axis=1)
    other = lax.dynamic_slice_in_dim(left, (1 - core) * height, height, axis=1)
    return (tn(own, right) + core_hop(tn(other, right).astype(BF16)).astype(F32)).astype(BF16)


def join_halves(pair_b, other, core):
    total = (pair_b.astype(F32) + other.astype(F32)).astype(BF16)
    back = core_hop(total)
    first = jnp.where(core == 0, total, back)
    second = jnp.where(core == 0, back, total)
    return jnp.concatenate([first, second]).astype(F32)


tie = lax.optimization_barrier


def tensor_split(
    tokens,
    segments,
    cotangent,
    qkv_weight,
    out_weight,
    gate_up_weight,
    down_weight,
    q_gain,
    k_gain,
    attn_gain,
    mlp_gain,
):
    members, copies = 8, 4
    rows = tokens.shape[0]
    count = members * rows
    wide = D // members
    units = FF // members
    quarter = units // copies
    place = lax.axis_index("fsdp")
    copy = lax.axis_index("replica")
    core = copy % 2
    owned = qkv_weight.shape[0]
    sub = owned // copies
    copy_at = copy.astype(jnp.int32).reshape(1)

    def qkv_block(k):
        parts = [
            lax.dynamic_slice(qkv_weight, (copy * sub, i * D + (place ^ k) * wide), (sub, wide))
            for i in range(3)
        ]
        return jnp.concatenate(parts, axis=1)

    def gate_up_block(member):
        parts = [
            lax.dynamic_slice_in_dim(
                gate_up_source, i * FF + member * units + copy * quarter, quarter, axis=1
            )
            for i in range(2)
        ]
        return jnp.concatenate(parts, axis=1)

    mine = lambda gain: lax.dynamic_slice_in_dim(gain, place * wide, wide)
    gain_own = jnp.stack([mine(q_gain), mine(k_gain)])

    qkv_blocks = swap_blocks(qkv_block)
    gate_up_source = gate_up_weight

    def early(s2, near):
        nonlocal gate_up_source
        s2, near, gate_up_source = tie((s2, near, gate_up_weight))
        return s2, near

    def late(far):
        nonlocal qkv_blocks
        far, qkv_blocks = tie((far, qkv_blocks))
        return far

    token_slots = spread(tokens, early, late)
    pieces = absolute(replica_gather(absolute(qkv_blocks, place)), copy)
    qkv_cols = pieces.transpose(1, 0, 2, 3).reshape(D, 3 * wide)
    cosine, sine = rope_tables(rows)
    sign = jnp.where(jnp.arange(HEAD_DIM) < HEAD_DIM // 2, -1.0, 1.0)
    cosine, sine = cosine[:, 0], sine[:, 0] * sign

    token_all = jnp.concatenate(token_slots)
    qkv = fold_with(token_all, qkv_cols)
    gate_up_piece = jnp.stack([gate_up_block(i) for i in range(members)])
    gate_up_piece = lax.all_to_all(gate_up_piece, "fsdp", 0, 0, tiled=True).reshape(D, 2 * quarter)

    q_pre, k_pre = (qkv[:, :wide], qkv[:, wide : 2 * wide])
    squares = [jnp.sum(value * value, axis=1).reshape(members, rows) for value in (q_pre, k_pre)]
    seg_rows = jnp.zeros((members, rows), F32).at[0].set(segments.astype(F32))
    factors = slot_mean(jnp.stack(squares + [seg_rows], axis=1), True)
    slab = lambda width, n=1: pl.BlockSpec((n * rows, width), lambda i: (i, 0))
    line = lambda height, n=1: pl.BlockSpec((n, height, rows), lambda i: (i, 0, 0))
    whole = lambda shape: pl.BlockSpec(shape, lambda i: (0,) * len(shape))
    tables = [whole((2, wide)), whole((rows, HEAD_DIM)), whole((rows, HEAD_DIM))]
    rot, attn_b = call(
        attend_body,
        (members // 2,),
        [slab(3 * wide, 2), line(3, 2)] + tables,
        [slab(3 * wide, 2), slab(wide, 2)],
        [jax.ShapeDtypeStruct((count, 3 * wide), BF16), jax.ShapeDtypeStruct((count, wide), BF16)],
        flops=4 * count * rows * wide,
        moved=count * wide * 20,
    )(qkv, factors, gain_own, cosine, sine)

    span = 2 * rows
    rows_of = lambda value, j: value[j * span : (j + 1) * span]
    pre_attn = collect(lambda j: fold_with(rows_of(attn_b, j), out_weight).reshape(2, rows, D))
    gate_up_all = replica_gather(gate_up_piece)
    mid = tokens.astype(F32) + pre_attn * rms_scale(pre_attn) * attn_gain
    mid_b = mid.astype(BF16)

    def late_mid(far):
        nonlocal gate_up_all
        far, gate_up_all = tie((far, gate_up_all))
        return far

    mid_all = jnp.concatenate(spread(mid_b, None, late_mid))
    gate_up_cols = jnp.zeros((D, 2 * units), BF16)
    for k, block in enumerate(gate_up_all):
        gate_up_cols = lax.dynamic_update_slice_in_dim(
            gate_up_cols, block, (copy ^ k) * 2 * quarter, axis=1
        )
    gate_up = fold_with(mid_all, gate_up_cols)
    strip = lambda i: gate_up[:, i * quarter : (i + 1) * quarter]
    gate = [strip(2 * c) for c in range(copies)]
    upper = [strip(2 * c + 1) for c in range(copies)]
    sigma = [jax.nn.sigmoid(value) for value in gate]
    hidden_b = jnp.concatenate(
        [(g * s * u).astype(BF16) for g, s, u in zip(gate, sigma, upper)], axis=1
    )
    pre_mlp = collect(lambda j: fold_with(rows_of(hidden_b, j), down_weight).reshape(2, rows, D))
    result = (mid + pre_mlp * rms_scale(pre_mlp) * mlp_gain).astype(BF16)
    d_pre_mlp, mlp_gain_part = rms_back(pre_mlp, mlp_gain, cotangent)
    dmlp_b = d_pre_mlp.astype(BF16)

    dmlp_all = jnp.concatenate(spread(dmlp_b))
    d_hidden = back_with(dmlp_all, down_weight)
    dgu = []
    for c in range(copies):
        d_h = d_hidden[:, c * quarter : (c + 1) * quarter]
        d_gate = d_h * upper[c] * sigma[c] * (1.0 + gate[c] * (1.0 - sigma[c]))
        d_upper = d_h * gate[c] * sigma[c]
        dgu += [d_gate.astype(BF16), d_upper.astype(BF16)]
    dgu = jnp.concatenate(dgu, axis=1)
    quarter_grad = lambda m: tn(
        mid_all, lax.dynamic_slice_in_dim(dgu_all, (copy ^ m) * 2 * quarter, 2 * quarter, axis=1)
    )
    dgu_all = dgu
    kept = {}

    def d_mid_step(j):
        nonlocal dgu
        if j == 1:
            pair = halves(hidden_b, dmlp_all, core, units // 2)
            dgu, kept["pair"] = tie((dgu, pair))
            kept["down"] = chip_hop(kept["pair"])
        if j == 0:
            sends = [quarter_grad(m).astype(BF16) for m in (3, 1)]
            dgu, *sends = tie((dgu, *sends))
            kept[3], kept[1] = (core_hop(value) for value in sends)
            sent = (quarter_grad(2) + kept[3].astype(F32)).astype(BF16)
            kept[2] = chip_hop(sent)
            kept[0] = quarter_grad(0) + kept[1].astype(F32)
        return back_with(rows_of(dgu, j), gate_up_cols).reshape(2, rows, D)

    d_mid = cotangent + collect(d_mid_step)
    d_mid, gate_up_own = tie((d_mid, kept[0]))
    down_pair, down_other = kept["pair"], kept["down"]
    gate_up_part = (gate_up_own + kept[2].astype(F32)).astype(BF16)

    d_pre_attn, attn_gain_part = rms_back(pre_attn, attn_gain, d_mid)
    dattn_all = jnp.concatenate(spread(d_pre_attn.astype(BF16)))
    dattn_all, gate_up_part = tie((dattn_all, gate_up_part))
    d_attn_b = back_with(dattn_all, out_weight).astype(BF16)
    gate_up_part = gate_up_part.reshape(members, owned, 2 * quarter)
    gate_up_part = lax.all_to_all(gate_up_part, "fsdp", 0, 0, tiled=True)
    attend_back = call(
        attend_back_body,
        (members // 2,),
        [slab(3 * wide, 2), slab(wide, 2), slab(3 * wide, 2), line(3, 2)] + tables,
        [slab(2 * wide, 2), slab(wide, 2), line(2, 2), whole((2, wide))],
        [
            jax.ShapeDtypeStruct((count, 2 * wide), F32),
            jax.ShapeDtypeStruct((count, wide), BF16),
            jax.ShapeDtypeStruct((members, 2, rows), F32),
            jax.ShapeDtypeStruct((2, wide), F32),
        ],
        flops=10 * count * rows * wide,
        moved=count * wide * 30,
    )
    d_norm, d_value, inner, gain_sums = attend_back(rot, d_attn_b, qkv, factors, gain_own, cosine, sine)
    inner, dattn_late = tie((inner, dattn_all))
    means = slot_mean(inner, False)
    means, down_pair = tie((means, down_pair))
    out_pair = halves(attn_b, dattn_late, core, wide // 2)
    out_other = chip_hop(out_pair)
    dqkv_b = call(
        norm_back_body,
        (members,),
        [slab(2 * wide), slab(wide), slab(3 * wide), line(3), line(2), whole((2, wide))],
        slab(3 * wide),
        jax.ShapeDtypeStruct((count, 3 * wide), BF16),
        flops=count * wide * 10,
        moved=count * wide * 28,
    )(d_norm, d_value, qkv, factors, means, gain_own)
    blank = jnp.zeros((2, D), F32)
    gains = jnp.concatenate(
        [
            lax.dynamic_update_slice_in_dim(blank, gain_sums, place * wide, axis=1),
            attn_gain_part[None],
            mlp_gain_part[None],
        ]
    )
    gains = gains + chip_hop(gains)
    gains = gains + core_hop(gains)
    for bits in (1, 2, 4):
        gains = gains + hop(gains, bits)
    down_grad = join_halves(down_pair, down_other, core)
    dqkv_b, out_other = tie((dqkv_b, out_other))

    qkv_full = tn(token_all, dqkv_b).reshape(members, copies, sub, 3 * wide)
    part_for = lambda m: lax.dynamic_index_in_dim(qkv_full, copy ^ m, axis=1, keepdims=False)
    third, first = part_for(3).astype(BF16), part_for(1).astype(BF16)
    dqkv_b, third, first = tie((dqkv_b, third, first))
    qkv_sent = (part_for(2) + core_hop(third).astype(F32)).astype(BF16)
    qkv_own = part_for(0) + core_hop(first).astype(F32)
    qkv_part = (qkv_own + chip_hop(qkv_sent).astype(F32)).astype(BF16)
    gate_up_parts = replica_gather(gate_up_part)
    qkv_blocks = swap_blocks(
        lambda k: lax.dynamic_index_in_dim(qkv_part, place ^ k, axis=0, keepdims=False)
    )
    input_grad = d_mid + collect(
        lambda j: back_with(rows_of(dqkv_b, j), qkv_cols).reshape(2, rows, D)
    )
    out_grad = join_halves(out_pair, out_other, core)
    gate_up_grad = call(
        gate_up_body,
        (2, members),
        [pl.BlockSpec((1, owned, quarter), lambda h, i, c: (i, 0, h))] * copies,
        pl.BlockSpec((owned, units), lambda h, i, c: (0, h * members + i)),
        jax.ShapeDtypeStruct((owned, 2 * FF), F32),
        moved=owned * FF * 12,
        scalars=1,
    )(copy_at, *gate_up_parts)
    qkv_blocks, out_grad, gains = tie((qkv_blocks, out_grad, gains))
    qkv_grad = call(
        qkv_body,
        (3,),
        [pl.BlockSpec((members, sub, wide), lambda i, c: (0, 0, i))] * copies,
        pl.BlockSpec((owned, D), lambda i, c: (0, i)),
        jax.ShapeDtypeStruct((owned, 3 * D), F32),
        moved=owned * D * 18,
        scalars=1,
    )(copy_at, *replica_gather(absolute(qkv_blocks, place)))
    return (
        result,
        input_grad,
        qkv_grad,
        out_grad,
        gate_up_grad,
        down_grad,
        gains[0],
        gains[1],
        gains[2],
        gains[3],
    )


def solution(mesh):
    def per_device(*arrays):
        fits = mesh.shape["fsdp"] == 8 and mesh.shape["replica"] == 4 and arrays[0].shape[0] == SEQ
        if not fits:
            return gathered(*arrays)
        return tensor_split(*arrays)


    placed = (
        P(("replica", "fsdp"), None),
        P(("replica", "fsdp")),
        P(("replica", "fsdp"), None),
        P("fsdp", None),
        P("fsdp", None),
        P("fsdp", None),
        P("fsdp", None),
        P(),
        P(),
        P(),
        P(),
    )
    return jax.shard_map(
        per_device,
        mesh=mesh,
        in_specs=placed,
        out_specs=(
            P(("replica", "fsdp"), None),
            P(("replica", "fsdp"), None),
            P("fsdp", None),
            P("fsdp", None),
            P("fsdp", None),
            P("fsdp", None),
            P(),
            P(),
            P(),
            P(),
        ),
        check_vma=False,
    )
```
